128 devices in a mesh: freq: 8 (over x, y_hi), trace: 16 (over y_lo, z, core).
Axes of the slice: x: 4, y: 4 (y_hi: 2, y_lo: 2; y = y_hi * 2 + y_lo), z: 4, core: 2. Of those that a mesh axis runs over, the one named last changes fastest.
Arguments:
- traces: float32 [256, 256, 2048], P(('freq', 'trace')), may hold values from -6 to 6
- source_weights: float32 [256, 256, 512], P(None, 'trace'), may hold values from -0.0625 to 0.0625
- level_weights: float32 [4, 4096, 1024], P(None, 'trace'), may hold values from -0.1875 to 0.1875
- slowness_weights: float32 [4096, 512], P('trace'), may hold values from -0.25 to 0.25
Outputs:
- radon_image: float32 [4096, 256], P(('trace', 'freq'))
The draws below stay inside these ranges and needn't reach their ends.
All inputs are finite; a program needn't handle non-finite values.
Results may differ from the reference program's by a relative error of at most 0.00011.
Values sent between devices are 32-bit elements; how exact they have to be, the bound alone decides.
No kernel may reach another device: no remote copies, remote signals or barrier semaphores. Data moves between devices by JAX's collectives and lax.ppermute only.
A program may use at most 128 MiB of HBM per device.

```python
import math
import jax
import jax.numpy as jnp
import numpy as np
from jax import lax

SAMPLES = 2048
FREQS = 1024
OFFSETS = 256
K = 256
SLOW = 4096
TAUS = 256
SHOTS = 256
BOXES = 16
LEVELS = 4


def steps_of(own_key, dims, cuts, smallest, largest):
    factor_of, own = 1.0, jax.random.fold_in(own_key, 6)
    for dim, shards_of in cuts:
        draws = jnp.exp(jax.random.uniform(jax.random.fold_in(own, dim), (shards_of,), jnp.float32, smallest / len(cuts), largest / len(cuts)))
        factor_of = factor_of * jnp.repeat(draws, dims[dim] // shards_of).reshape([-1 if axis == dim else 1 for axis in range(len(dims))])
    return factor_of


def gaussian(stream_key, extent, deviation, bound, shards=(), kind=jnp.bfloat16):
    entries = jax.random.normal(stream_key, extent, jnp.float32) * deviation
    if len(shards) > 0:
        entries = steps_of(stream_key, extent, shards, -0.22, 0.18) * entries
    return jnp.clip(entries, min=-bound, max=bound).astype(kind)


def setup_inputs(seed: int = 0) -> dict:
    key_list = jax.random.split(jax.random.key(seed), 5)
    return {
        "traces": gaussian(key_list[0], (SHOTS, OFFSETS, SAMPLES), 1.0, 6.0, ((0, 128),), jnp.float32),
        "source_weights": gaussian(key_list[1], (SHOTS, OFFSETS, 2 * K), (2 * SHOTS * OFFSETS // BOXES) ** -0.5, 0.0625, ((1, 16),), jnp.float32),
        "level_weights": gaussian(key_list[2], (LEVELS, BOXES * K, 4 * K), (4 * K) ** -0.5, 0.1875, ((1, 16),), jnp.float32),
        "slowness_weights": gaussian(key_list[3], (SLOW, 2 * K), (2 * K) ** -0.5, 0.25, ((0, 16),), jnp.float32),
    }


def contract_box(weights, values):
    return jnp.einsum('sbok,sbof->bkf', weights, values, precision=lax.Precision.HIGHEST)

def apply_box(weights, values):
    return jnp.einsum('bkj,bjf->bkf', weights, values, precision=lax.Precision.HIGHEST)

def reference(traces, source_weights, level_weights, slowness_weights):
    spectrum = jnp.fft.rfft(traces, axis=-1)[..., :FREQS] / math.sqrt(SAMPLES)
    box_offsets = OFFSETS // BOXES
    spec_real = jnp.real(spectrum).astype(jnp.float32).reshape(SHOTS, BOXES, box_offsets, FREQS)
    spec_imag = jnp.imag(spectrum).astype(jnp.float32).reshape(SHOTS, BOXES, box_offsets, FREQS)
    sources = source_weights.reshape(SHOTS, BOXES, box_offsets, 2 * K)
    src_real = sources[..., :K]
    src_imag = sources[..., K:]
    coeff_real = contract_box(src_real, spec_real) - contract_box(src_imag, spec_imag)
    coeff_imag = contract_box(src_real, spec_imag) + contract_box(src_imag, spec_real)
    weights_all = level_weights.reshape(LEVELS, BOXES, K, 4 * K)
    box_ids = np.arange(BOXES)
    for level_no in range(LEVELS):
        partner = box_ids ^ 1 << level_no
        part_real = coeff_real[partner]
        part_imag = coeff_imag[partner]
        weights = weights_all[level_no]
        own_real = weights[..., :K]
        par_real = weights[..., K:2 * K]
        own_imag = weights[..., 2 * K:3 * K]
        par_imag = weights[..., 3 * K:]
        new_real = apply_box(own_real, coeff_real) - apply_box(own_imag, coeff_imag) + apply_box(par_real, part_real) - apply_box(par_imag, part_imag)
        new_imag = apply_box(own_real, coeff_imag) + apply_box(own_imag, coeff_real) + apply_box(par_real, part_imag) + apply_box(par_imag, part_real)
        coeff_real, coeff_imag = (new_real, new_imag)
    evaluate = slowness_weights.reshape(BOXES, SLOW // BOXES, 2 * K)
    eval_real = evaluate[..., :K]
    eval_imag = evaluate[..., K:]
    image_real = apply_box(eval_real, coeff_real) - apply_box(eval_imag, coeff_imag)
    image_imag = apply_box(eval_real, coeff_imag) + apply_box(eval_imag, coeff_real)
    tau_ids = jnp.arange(TAUS, dtype=jnp.int32) * (SAMPLES // (4 * TAUS))
    freq_ids = jnp.arange(FREQS, dtype=jnp.int32)
    turns = (freq_ids[:, None] * tau_ids[None, :] % SAMPLES).astype(jnp.float32) * (2.0 * math.pi / SAMPLES)
    cosines = jnp.cos(turns)
    sines = jnp.sin(turns)
    radon_image = (jnp.einsum('bpf,ft->bpt', image_real, cosines, precision=lax.Precision.HIGHEST) - jnp.einsum('bpf,ft->bpt', image_imag, sines, precision=lax.Precision.HIGHEST)) / math.sqrt(FREQS)
    return radon_image.reshape(SLOW, TAUS)
```

```python
import functools
import math

import jax
import jax.numpy as jnp
import numpy as np
from jax import lax
from jax.experimental import pallas as pl
from jax.experimental.pallas import tpu as pltpu
from jax.sharding import PartitionSpec as P

FREQS = 1024
TAUS = 256
F32 = jnp.float32
BF16 = jnp.bfloat16
NT = (((1,), (1,)), ((), ()))
NN = (((1,), (0,)), ((), ()))


def split(x):
    high = x.astype(BF16)
    return high, (x - high.astype(F32)).astype(BF16)


def mm(a, b, dims):
    return lax.dot_general(a, b, dims, preferred_element_type=F32)


def mm3(a_pair, b_pair, dims):
    rows = a_pair[0].shape[0]
    both = mm(jnp.concatenate(a_pair, axis=0), b_pair[0], dims)
    return both[:rows] + both[rows:] + mm(a_pair[0], b_pair[1], dims)


def tau_order(freq_count):
    per = TAUS // freq_count
    columns = np.arange(TAUS)
    owner, inner = columns // per, columns % per
    return (inner // 8) * (8 * freq_count) + owner * 8 + inner % 8


def tables(samples, freq_count):
    taus = tau_order(freq_count)
    step = samples // (4 * TAUS)
    scale = 1.0 / math.sqrt(samples) / math.sqrt(FREQS)
    n = np.arange(samples)[:, None]
    gap = (step * taus[None, :] - n) % samples
    odd = gap % 2 == 1
    cot = np.where(odd, 1.0 / np.tan(np.pi * np.where(odd, gap, 1) / samples), 0.0) * scale
    cot = cot.astype(np.float32)
    high = cot.astype(jnp.bfloat16)
    low = (cot - high.astype(np.float32)).astype(jnp.bfloat16)
    pick = (gap[: samples // 4] == 0).astype(jnp.bfloat16)
    return high, low, pick, FREQS * scale, scale


def move_groups(parts, width):
    count = len(parts)
    lanes = count * width
    group = lax.broadcasted_iota(jnp.int32, parts[0].shape, 1) // width
    turned = [p if x == 0 else pltpu.roll(p, width * x, 1) for x, p in enumerate(parts)]
    result = []
    for q in range(count):
        got = turned[(-q) % count]
        for spot in range(1, count):
            got = jnp.where(group == spot, turned[(spot - q) % count], got)
        result.append(got if q == 0 else pltpu.roll(got, lanes - width * q, 1))
    return result


def trace_kernel(keep, tone, x_ref, high_ref, low_ref, pick_ref, out_ref):
    rows = x_ref.shape[1]
    x = jnp.concatenate([x_ref[0], x_ref[1]], axis=0)
    total = x[:, :128]
    for at in range(128, x.shape[1], 128):
        total = total + x[:, at : at + 128]
    odd = lax.broadcasted_iota(jnp.int32, total.shape, 1) % 2 == 1
    mean = jnp.sum(jnp.where(odd, total, 0.0), axis=1, keepdims=True) * tone
    pair = split(x)
    imag = mm3(pair, (high_ref[...], low_ref[...]), NN)
    head = pick_ref.shape[0]
    both = mm(jnp.concatenate([p[:, :head] for p in pair], axis=0), pick_ref[...], NN)
    real = (both[: 2 * rows] + both[2 * rows :]) * keep + mean
    for tile in range(TAUS // 128):
        lanes = slice(128 * tile, 128 * tile + 128)
        parts = [real[:rows, lanes], imag[:rows, lanes], real[rows:, lanes], imag[rows:, lanes]]
        for q, block in enumerate(move_groups(parts, 32)):
            out_ref[4 * tile + q] = block.reshape(out_ref.shape[1:])


def trace_blocks(traces, freq_count, trace_count):
    shots, offsets, samples = traces.shape
    box = offsets // trace_count
    steps = 4
    high, low, pick, keep, tone = tables(samples, freq_count)
    whole = lambda a: pl.BlockSpec(a.shape, lambda i: (0, 0))
    return pl.pallas_call(
        functools.partial(trace_kernel, keep, tone),
        grid=(steps,),
        in_specs=[
            pl.BlockSpec((shots, offsets // steps, samples), lambda i: (0, i, 0)),
            whole(high),
            whole(low),
            whole(pick),
        ],
        out_specs=pl.BlockSpec(
            (freq_count, trace_count // steps, box, 128), lambda i: (0, i, 0, 0)
        ),
        out_shape=jax.ShapeDtypeStruct((freq_count, trace_count, box, 128), F32),
        compiler_params=pltpu.CompilerParams(vmem_limit_bytes=32 << 20),
        name="trace_blocks",
    )(traces, jnp.asarray(high), jnp.asarray(low), jnp.asarray(pick))


def gram_kernel(values_ref, source_ref, out_ref, acc_ref):
    step = pl.program_id(0)
    depth = values_ref.shape[0] * values_ref.shape[1]
    turned = values_ref[...].reshape(depth, 128).T
    pair = split(turned)
    source = source_ref[...]
    source = source.reshape(source.shape[0] // 2, 2, *source.shape[1:])
    acc = None
    for shot in range(2):
        rows = slice(64 * shot, 64 * shot + 64)
        weights = split(source[:, shot].reshape(depth, source.shape[3]))
        term = mm3((pair[0][rows], pair[1][rows]), weights, NN)
        acc = term if acc is None else acc + term

    @pl.when(step == 0)
    def _():
        acc_ref[...] = acc

    @pl.when(step > 0)
    def _():
        acc_ref[...] += acc

    @pl.when(step == pl.num_programs(0) - 1)
    def _():
        out_ref[...] = turn(acc_ref[...])


def turn(both):
    half, width = both.shape[0] // 2, both.shape[1] // 2
    real = both[:half, :width] - both[half:, width:]
    imag = both[half:, :width] + both[:half, width:]
    return jnp.concatenate([real, imag], axis=0)


def gram(values, sources):
    senders, box, lanes = values.shape
    shots, _, width = sources.shape
    steps = 4
    return pl.pallas_call(
        gram_kernel,
        grid=(steps,),
        in_specs=[
            pl.BlockSpec((senders // steps, box, lanes), lambda i: (i, 0, 0)),
            pl.BlockSpec((shots // steps, box, width), lambda i: (i, 0, 0)),
        ],
        out_specs=pl.BlockSpec((64, width // 2), lambda i: (0, 0)),
        out_shape=jax.ShapeDtypeStruct((64, width // 2), F32),
        scratch_shapes=[pltpu.VMEM((64, width), F32)],
        compiler_params=pltpu.CompilerParams(vmem_limit_bytes=32 << 20),
        name="gram",
    )(values, sources)


def own_kernel(c_ref, w_ref, own_ref, high_ref, low_ref):
    k = c_ref.shape[1]
    weights = w_ref[0]
    own = split(jnp.concatenate([weights[:, :k], weights[:, 2 * k : 3 * k]], axis=0))
    own_ref[...] = turn(mm3(split(c_ref[...]), own, NT))
    high, low = split(jnp.concatenate([weights[:, k : 2 * k], weights[:, 3 * k :]], axis=0))
    high_ref[...] = high
    low_ref[...] = low


def own_part(c, weights, level):
    rows, k = c.shape
    return pl.pallas_call(
        own_kernel,
        grid=(1,),
        in_specs=[
            pl.BlockSpec((rows, k), lambda i: (0, 0)),
            pl.BlockSpec((1, k, 4 * k), lambda i: (level, 0, 0)),
        ],
        out_specs=[
            pl.BlockSpec((rows, k), lambda i: (0, 0)),
            pl.BlockSpec((2 * k, k), lambda i: (0, 0)),
            pl.BlockSpec((2 * k, k), lambda i: (0, 0)),
        ],
        out_shape=[
            jax.ShapeDtypeStruct((rows, k), F32),
            jax.ShapeDtypeStruct((2 * k, k), BF16),
            jax.ShapeDtypeStruct((2 * k, k), BF16),
        ],
        compiler_params=pltpu.CompilerParams(vmem_limit_bytes=16 << 20),
        cost_estimate=pl.CostEstimate(flops=10**8, bytes_accessed=10**6, transcendentals=0),
        name="own_part",
    )(c, weights)


def joined(own_ref, c_ref, high_ref, low_ref):
    return own_ref[...] + turn(mm3(split(c_ref[...]), (high_ref[...], low_ref[...]), NT))


def join_kernel(own_ref, c_ref, high_ref, low_ref, out_ref):
    out_ref[...] = joined(own_ref, c_ref, high_ref, low_ref)


def last_kernel(own_ref, c_ref, high_ref, low_ref, e_ref, out_ref):
    c = joined(own_ref, c_ref, high_ref, low_ref)
    half = c.shape[0] // 2
    row = jnp.concatenate([c[:half], -c[half:]], axis=1)
    values = mm3(split(row), split(e_ref[...]), NT)
    for tile in range(values.shape[1] // 128):
        lanes = slice(128 * tile, 128 * tile + 128)
        parts = [values[8 * g : 8 * g + 8, lanes] for g in range(4)]
        for q, block in enumerate(move_groups(parts, 32)):
            out_ref[4 * tile + q] = block


def join_part(own, c, high, low):
    return pl.pallas_call(
        join_kernel,
        out_shape=jax.ShapeDtypeStruct(c.shape, F32),
        compiler_params=pltpu.CompilerParams(vmem_limit_bytes=16 << 20),
        name="join_part",
    )(own, c, high, low)


def last_part(own, c, high, low, e, freq_count):
    return pl.pallas_call(
        last_kernel,
        out_shape=jax.ShapeDtypeStruct((freq_count, 8, 128), F32),
        compiler_params=pltpu.CompilerParams(vmem_limit_bytes=16 << 20),
        name="last_part",
    )(own, c, high, low, e)


def final_kernel(x_ref, out_ref):
    x = x_ref[...].reshape(-1, 128)
    x = jnp.concatenate([x, jnp.zeros_like(x)], axis=0).T
    low = lax.broadcasted_iota(jnp.int32, (32, 128), 1) < 64
    for tile in range(2):
        first = x[64 * tile : 64 * tile + 32]
        second = x[64 * tile + 32 : 64 * tile + 64]
        out_ref[:, 128 * tile : 128 * tile + 128] = jnp.where(
            low, first, pltpu.roll(second, 64, 1)
        )


def final_part(x):
    return pl.pallas_call(
        final_kernel,
        out_shape=jax.ShapeDtypeStruct((32, TAUS), F32),
        compiler_params=pltpu.CompilerParams(vmem_limit_bytes=16 << 20),
        name="final_part",
    )(x)


def from_partner(block, axis, apart):
    count = lax.axis_size(axis)
    return lax.ppermute(block, axis, [(at, at ^ (1 << apart)) for at in range(count)])


def body(traces, source_weights, level_weights, slowness_weights):
    freq_count = lax.axis_size("freq")
    trace_count = lax.axis_size("trace")
    blocks = trace_blocks(traces, freq_count, trace_count)
    blocks = blocks.reshape(freq_count * trace_count, *blocks.shape[2:])
    values = lax.all_to_all(blocks, ("freq", "trace"), split_axis=0, concat_axis=0, tiled=True)
    c = gram(values, source_weights)
    levels = level_weights.shape[0]
    for level in range(levels):
        partner = from_partner(c, "trace", level)
        own, high, low = own_part(c, level_weights, level)
        if level < levels - 1:
            c = join_part(own, partner, high, low)
        else:
            out = last_part(own, partner, high, low, slowness_weights, freq_count)
    out = lax.all_to_all(out, "freq", split_axis=0, concat_axis=0, tiled=True)
    return final_part(out)


def solution(mesh):
    return jax.shard_map(
        body,
        mesh=mesh,
        in_specs=(
            P(("freq", "trace"), None, None),
            P(None, "trace", None),
            P(None, "trace", None),
            P("trace", None),
        ),
        out_specs=P(("trace", "freq"), None),
        check_vma=False,
    )
```

```python
import functools
import math

import jax
import jax.numpy as jnp
import numpy as np
from jax import lax
from jax.experimental import pallas as pl
from jax.experimental.pallas import tpu as pltpu
from jax.sharding import PartitionSpec as P

FREQS = 1024
TAUS = 256
F32 = jnp.float32
BF16 = jnp.bfloat16
NT = (((1,), (1,)), ((), ()))
NN = (((1,), (0,)), ((), ()))


def split(x):
    high = x.astype(BF16)
    return high, (x - high.astype(F32)).astype(BF16)


def mm(a, b, dims):
    return lax.dot_general(a, b, dims, preferred_element_type=F32)


def mm3(a_pair, b_pair, dims):
    rows = a_pair[0].shape[0]
    both = mm(jnp.concatenate(a_pair, axis=0), b_pair[0], dims)
    return both[:rows] + both[rows:] + mm(a_pair[0], b_pair[1], dims)


def tau_order(freq_count):
    per = TAUS // freq_count
    columns = np.arange(TAUS)
    owner, inner = columns // per, columns % per
    return (inner // 8) * (8 * freq_count) + owner * 8 + inner % 8


def tables(samples, freq_count):
    taus = tau_order(freq_count)
    step = samples // (4 * TAUS)
    scale = 1.0 / math.sqrt(samples) / math.sqrt(FREQS)
    n = np.arange(samples)[:, None]
    gap = (step * taus[None, :] - n) % samples
    odd = gap % 2 == 1
    cot = np.where(odd, 1.0 / np.tan(np.pi * np.where(odd, gap, 1) / samples), 0.0) * scale
    cot = cot.astype(np.float32)
    high = cot.astype(jnp.bfloat16)
    low = (cot - high.astype(np.float32)).astype(jnp.bfloat16)
    pick = (gap[: samples // 4] == 0).astype(jnp.bfloat16)
    return high, low, pick, FREQS * scale, scale


def move_groups(parts, width):
    count = len(parts)
    lanes = count * width
    group = lax.broadcasted_iota(jnp.int32, parts[0].shape, 1) // width
    turned = [p if x == 0 else pltpu.roll(p, width * x, 1) for x, p in enumerate(parts)]
    result = []
    for q in range(count):
        got = turned[(-q) % count]
        for spot in range(1, count):
            got = jnp.where(group == spot, turned[(spot - q) % count], got)
        result.append(got if q == 0 else pltpu.roll(got, lanes - width * q, 1))
    return result


def trace_kernel(keep, tone, freq_count, x_hbm, high_hbm, low_hbm, pick_hbm, out_ref, *scratch):
    x_ref, high_ref, low_ref, pick_ref, imag_ref, real_ref, total_ref, x_sem, table_sem = scratch
    shots, offsets, samples = x_hbm.shape
    rows = shots * offsets
    wide = x_ref.shape[2]
    count = samples // wide
    heads = pick_hbm.shape[0] // wide
    copies = []
    for at in range(count):
        part = pl.ds(at * wide, wide)
        group = [
            pltpu.make_async_copy(x_hbm.at[s, :, part], x_ref.at[at, pl.ds(s * offsets, offsets)], x_sem.at[at, s])
            for s in range(shots)
        ]
        group.append(pltpu.make_async_copy(high_hbm.at[part], high_ref.at[part], table_sem.at[at, 0]))
        group.append(pltpu.make_async_copy(low_hbm.at[part], low_ref.at[part], table_sem.at[at, 1]))
        if at < heads:
            group.append(
                pltpu.make_async_copy(pick_hbm.at[part], pick_ref.at[part], table_sem.at[at, 2])
            )
        copies.append(group)
        for copy in group:
            copy.start()
    for at in range(count):
        part = slice(at * wide, at * wide + wide)
        for copy in copies[at]:
            copy.wait()
        x = x_ref[at]
        total = x[:, :128]
        for lane in range(128, wide, 128):
            total = total + x[:, lane : lane + 128]
        pair = split(x)
        imag = mm3(pair, (high_ref[part], low_ref[part]), NN)
        if at < heads:
            both = mm(jnp.concatenate(pair, axis=0), pick_ref[part], NN)
            real = (both[:rows] + both[rows:]) * keep
        if at == 0:
            imag_ref[...] = imag
            real_ref[...] = real
            total_ref[...] = total
        else:
            imag_ref[...] += imag
            total_ref[...] += total
            if at < heads:
                real_ref[...] += real
    total = total_ref[...]
    odd = lax.broadcasted_iota(jnp.int32, total.shape, 1) % 2 == 1
    real_ref[...] += jnp.sum(jnp.where(odd, total, 0.0), axis=1, keepdims=True) * tone
    core = lax.axis_index("trace") % 2
    pairs, _, box, lanes = out_ref.shape
    boxes = offsets // box
    for tile in range(TAUS // 128):
        cols = slice(128 * tile, 128 * tile + 128)
        parts = []
        for s in range(shots):
            own = slice(s * offsets, s * offsets + offsets)
            parts += [real_ref[own, cols], imag_ref[own, cols]]
        for q, block in enumerate(move_groups(parts, 32)):
            block = block.reshape(boxes // 2, 2, box, lanes)
            first = (4 * tile + q) * (boxes // 2)
            for side in range(2):
                out_ref[pl.ds(first, boxes // 2), side ^ core] = block[:, side]


def trace_blocks(traces, freq_count, trace_count):
    shots, offsets, samples = traces.shape
    box = offsets // trace_count
    wide = 256
    rows = shots * offsets
    high, low, pick, keep, tone = tables(samples, freq_count)
    return pl.pallas_call(
        functools.partial(trace_kernel, keep, tone, freq_count),
        in_specs=[pl.BlockSpec(memory_space=pltpu.HBM)] * 4,
        out_specs=pl.BlockSpec(memory_space=pltpu.VMEM),
        out_shape=jax.ShapeDtypeStruct((freq_count * trace_count // 2, 2, box, 128), F32),
        scratch_shapes=[
            pltpu.VMEM((samples // wide, rows, wide), F32),
            pltpu.VMEM(high.shape, BF16),
            pltpu.VMEM(low.shape, BF16),
            pltpu.VMEM(pick.shape, BF16),
            pltpu.VMEM((rows, TAUS), F32),
            pltpu.VMEM((rows, TAUS), F32),
            pltpu.VMEM((rows, 128), F32),
            pltpu.SemaphoreType.DMA((samples // wide, shots)),
            pltpu.SemaphoreType.DMA((samples // wide, 3)),
        ],
        compiler_params=pltpu.CompilerParams(vmem_limit_bytes=58 << 20),
        name="trace_blocks",
    )(traces, jnp.asarray(high), jnp.asarray(low), jnp.asarray(pick))


def gram_kernel(values_ref, source_ref, before_ref, out_ref, acc_ref):
    step = pl.program_id(0)
    depth = values_ref.shape[0] * values_ref.shape[2]
    pair = split(values_ref[...].reshape(depth, 128).T)
    source = source_ref[...]
    acc = None
    for shot in range(2):
        rows = slice(64 * shot, 64 * shot + 64)
        weights = split(source[:, 0, shot].reshape(depth, source.shape[4]))
        term = mm3((pair[0][rows], pair[1][rows]), weights, NN)
        acc = term if acc is None else acc + term

    @pl.when(step == 0)
    def _():
        acc_ref[...] = acc

    @pl.when(step > 0)
    def _():
        acc_ref[...] += acc

    @pl.when(step == pl.num_programs(0) - 1)
    def _():
        both = turn(acc_ref[...])
        out_ref[...] = both if before_ref is None else both + before_ref[...]


def gram(values, sources, core, before):
    senders, _, box, lanes = values.shape
    width = sources.shape[4]
    steps = 4
    start = before is None
    kernel = gram_kernel
    in_specs = [
        pl.BlockSpec((senders // steps, 1, box, lanes), lambda i, c: (i, 0, 0, 0)),
        pl.BlockSpec((senders // steps, 1, 2, box, width), lambda i, c: (i, c[0], 0, 0, 0)),
    ]
    if start:
        kernel = lambda c, v, s, o, a: gram_kernel(v, s, None, o, a)
    else:
        kernel = lambda c, v, s, b, o, a: gram_kernel(v, s, b, o, a)
        in_specs.append(pl.BlockSpec((64, width // 2), lambda i, c: (0, 0)))
    return pl.pallas_call(
        kernel,
        grid_spec=pltpu.PrefetchScalarGridSpec(
            num_scalar_prefetch=1,
            grid=(steps,),
            in_specs=in_specs,
            out_specs=pl.BlockSpec((64, width // 2), lambda i, c: (0, 0)),
            scratch_shapes=[pltpu.VMEM((64, width), F32)],
        ),
        out_shape=jax.ShapeDtypeStruct((64, width // 2), F32),
        compiler_params=pltpu.CompilerParams(vmem_limit_bytes=53 << 20),
        cost_estimate=pl.CostEstimate(flops=2 * 10**9, bytes_accessed=10**7, transcendentals=0),
        name="gram_first" if start else "gram_second",
    )(core, values, sources, *(() if start else (before,)))


def turn(both):
    half, width = both.shape[0] // 2, both.shape[1] // 2
    real = both[:half, :width] - both[half:, width:]
    imag = both[half:, :width] + both[:half, width:]
    return jnp.concatenate([real, imag], axis=0)


def own_kernel(c_ref, w_ref, own_ref, high_ref, low_ref):
    k = c_ref.shape[1]
    weights = w_ref[0]
    own = split(jnp.concatenate([weights[:, :k], weights[:, 2 * k : 3 * k]], axis=0))
    own_ref[...] = turn(mm3(split(c_ref[...]), own, NT))
    high, low = split(jnp.concatenate([weights[:, k : 2 * k], weights[:, 3 * k :]], axis=0))
    high_ref[...] = high
    low_ref[...] = low


def own_part(c, weights, level):
    rows, k = c.shape
    return pl.pallas_call(
        own_kernel,
        grid=(1,),
        in_specs=[
            pl.BlockSpec((rows, k), lambda i: (0, 0)),
            pl.BlockSpec((1, k, 4 * k), lambda i: (level, 0, 0)),
        ],
        out_specs=[
            pl.BlockSpec((rows, k), lambda i: (0, 0)),
            pl.BlockSpec((2 * k, k), lambda i: (0, 0)),
            pl.BlockSpec((2 * k, k), lambda i: (0, 0)),
        ],
        out_shape=[
            jax.ShapeDtypeStruct((rows, k), F32),
            jax.ShapeDtypeStruct((2 * k, k), BF16),
            jax.ShapeDtypeStruct((2 * k, k), BF16),
        ],
        compiler_params=pltpu.CompilerParams(vmem_limit_bytes=16 << 20),
        cost_estimate=pl.CostEstimate(flops=10**8, bytes_accessed=10**6, transcendentals=0),
        name="own_part",
    )(c, weights)


def joined(own_ref, c_ref, high_ref, low_ref):
    return own_ref[...] + turn(mm3(split(c_ref[...]), (high_ref[...], low_ref[...]), NT))


def join_kernel(own_ref, c_ref, high_ref, low_ref, out_ref):
    out_ref[...] = joined(own_ref, c_ref, high_ref, low_ref)


def last_kernel(own_ref, c_ref, high_ref, low_ref, e_ref, out_ref):
    c = joined(own_ref, c_ref, high_ref, low_ref)
    half = c.shape[0] // 2
    row = jnp.concatenate([c[:half], -c[half:]], axis=1)
    values = mm3(split(row), split(e_ref[...]), NT)
    for tile in range(values.shape[1] // 128):
        lanes = slice(128 * tile, 128 * tile + 128)
        parts = [values[8 * g : 8 * g + 8, lanes] for g in range(4)]
        for q, block in enumerate(move_groups(parts, 32)):
            out_ref[4 * tile + q] = block


def join_part(own, c, high, low):
    return pl.pallas_call(
        join_kernel,
        out_shape=jax.ShapeDtypeStruct(c.shape, F32),
        compiler_params=pltpu.CompilerParams(vmem_limit_bytes=16 << 20),
        name="join_part",
    )(own, c, high, low)


def last_part(own, c, high, low, e, freq_count):
    return pl.pallas_call(
        last_kernel,
        out_shape=jax.ShapeDtypeStruct((freq_count, 8, 128), F32),
        compiler_params=pltpu.CompilerParams(vmem_limit_bytes=16 << 20),
        name="last_part",
    )(own, c, high, low, e)


def final_kernel(x_ref, out_ref):
    x = x_ref[...].reshape(-1, 128)
    x = jnp.concatenate([x, jnp.zeros_like(x)], axis=0).T
    low = lax.broadcasted_iota(jnp.int32, (32, 128), 1) < 64
    for tile in range(2):
        first = x[64 * tile : 64 * tile + 32]
        second = x[64 * tile + 32 : 64 * tile + 64]
        out_ref[:, 128 * tile : 128 * tile + 128] = jnp.where(
            low, first, pltpu.roll(second, 64, 1)
        )


def final_part(x):
    return pl.pallas_call(
        final_kernel,
        out_shape=jax.ShapeDtypeStruct((32, TAUS), F32),
        compiler_params=pltpu.CompilerParams(vmem_limit_bytes=16 << 20),
        name="final_part",
    )(x)


def from_partner(block, axis, apart):
    count = lax.axis_size(axis)
    return lax.ppermute(block, axis, [(at, at ^ (1 << apart)) for at in range(count)])


def body(traces, source_weights, level_weights, slowness_weights):
    freq_count = lax.axis_size("freq")
    trace_count = lax.axis_size("trace")
    blocks = trace_blocks(traces, freq_count, trace_count)
    every = range(freq_count * trace_count)
    groups = [[d for d in every if d % 2 == side] for side in range(2)]
    blocks = lax.all_to_all(
        blocks, ("freq", "trace"), 0, 0, axis_index_groups=groups, tiled=True
    )
    crossed = from_partner(blocks[:, 1:], "trace", 0)
    core = (lax.axis_index("trace") % 2).reshape(1)
    sources = source_weights.reshape(blocks.shape[0], 2, 2, *source_weights.shape[1:])
    c = gram(blocks[:, :1], sources, core, None)
    c = gram(crossed, sources, 1 - core, c)
    levels = level_weights.shape[0]
    for level in range(levels):
        partner = from_partner(c, "trace", level)
        own, high, low = own_part(c, level_weights, level)
        if level < levels - 1:
            c = join_part(own, partner, high, low)
        else:
            out = last_part(own, partner, high, low, slowness_weights, freq_count)
    out = lax.all_to_all(out, "freq", split_axis=0, concat_axis=0, tiled=True)
    return final_part(out)


def solution(mesh):
    return jax.shard_map(
        body,
        mesh=mesh,
        in_specs=(
            P(("freq", "trace"), None, None),
            P(None, "trace", None),
            P(None, "trace", None),
            P("trace", None),
        ),
        out_specs=P(("trace", "freq"), None),
        check_vma=False,
    )
```

```python
import functools
import math

import jax
import jax.numpy as jnp
import numpy as np
from jax import lax
from jax.experimental import pallas as pl
from jax.experimental.pallas import tpu as pltpu
from jax.sharding import PartitionSpec as P

FREQS = 1024
TAUS = 256
F32 = jnp.float32
BF16 = jnp.bfloat16
NT = (((1,), (1,)), ((), ()))
NN = (((1,), (0,)), ((), ()))


def split(x):
    high = x.astype(BF16)
    return high, (x - high.astype(F32)).astype(BF16)


def mm(a, b, dims):
    return lax.dot_general(a, b, dims, preferred_element_type=F32)


def mm3(a_pair, b_pair, dims):
    rows = a_pair[0].shape[0]
    both = mm(jnp.concatenate(a_pair, axis=0), b_pair[0], dims)
    return both[:rows] + both[rows:] + mm(a_pair[0], b_pair[1], dims)


def lane_tau(lane):
    return 64 * (lane % 16 // 8) + 8 * (lane // 16) + lane % 8


def cot_table(samples, wide, scale):
    step = samples // (4 * TAUS)
    taus = lane_tau(np.arange(128))
    gap = wide * np.arange(samples // wide)[:, None, None] + step * taus
    gap = gap - (2 * np.arange(wide // 2)[None, :, None] + 1)
    return (scale / np.tan(np.pi * gap / samples)).astype(np.float32)


def move_groups(parts, width):
    count = len(parts)
    lanes = count * width
    group = lax.broadcasted_iota(jnp.int32, parts[0].shape, 1) // width
    turned = [p if x == 0 else pltpu.roll(p, width * x, 1) for x, p in enumerate(parts)]
    result = []
    for q in range(count):
        got = turned[(-q) % count]
        for spot in range(1, count):
            got = jnp.where(group == spot, turned[(spot - q) % count], got)
        result.append(got if q == 0 else pltpu.roll(got, lanes - width * q, 1))
    return result


def trace_kernel(scale, x_hbm, table_hbm, out_ref, x_ref, table_ref, full_ref, x_sem, table_sem):
    shots, offsets, samples = x_hbm.shape
    count, wide, _ = full_ref.shape
    rows = shots * offsets
    copies = [
        pltpu.make_async_copy(x_hbm.at[s], x_ref.at[pl.ds(s * offsets, offsets)], x_sem.at[s])
        for s in range(shots)
    ]
    table_copy = pltpu.make_async_copy(table_hbm, table_ref, table_sem)
    table_copy.start()
    for copy in copies:
        copy.start()
    lane = lax.broadcasted_iota(jnp.int32, (wide, 128), 1)
    row = lax.broadcasted_iota(jnp.int32, (wide, 128), 0)
    step = samples // (4 * TAUS)
    pick = jnp.where(row == step * lane_tau(lane), 1.0, 0.0).astype(BF16)
    full_ref[...] = jnp.zeros_like(full_ref)
    table_copy.wait()
    for d in range(count):
        full_ref[d, pl.ds(1, wide // 2, 2), :] = table_ref[d]
    table = [split(full_ref[d]) for d in range(count)]
    right = [
        jnp.concatenate(
            [
                jnp.concatenate([table[-at % count][part], table[(1 - at) % count][part]], axis=1)
                for at in range(count)
            ],
            axis=0,
        )
        for part in range(2)
    ]
    for copy in copies:
        copy.wait()
    x = x_ref[...]
    total = x[:, :128]
    for at in range(128, samples, 128):
        total = total + x[:, at : at + 128]
    pair = split(x)
    imag = mm3(pair, right, NN)
    odd = lax.broadcasted_iota(jnp.int32, total.shape, 1) % 2 == 1
    mean = jnp.sum(jnp.where(odd, total, 0.0), axis=1, keepdims=True) * scale
    real = []
    for half in range(2):
        part = slice(half * wide, half * wide + wide)
        both = mm(jnp.concatenate([p[:, part] for p in pair], axis=0), pick, NN)
        real.append((both[:rows] + both[rows:]) * (FREQS * scale) + mean)
    parts = []
    for s in range(shots):
        own = slice(s * offsets, s * offsets + offsets)
        parts += [real[0][own], real[1][own], imag[own, :128], imag[own, 128:]]
    for r, block in enumerate(move_groups(parts, 16)):
        out_ref[r] = block.reshape(out_ref.shape[1:])


def trace_blocks(traces, freq_count, trace_count):
    shots, offsets, samples = traces.shape
    wide = samples // 8
    scale = 1.0 / math.sqrt(samples) / math.sqrt(FREQS)
    table = jnp.asarray(cot_table(samples, wide, scale))
    return pl.pallas_call(
        functools.partial(trace_kernel, scale),
        in_specs=[pl.BlockSpec(memory_space=pltpu.HBM)] * 2,
        out_specs=pl.BlockSpec(memory_space=pltpu.VMEM),
        out_shape=jax.ShapeDtypeStruct(
            (freq_count, trace_count, offsets // trace_count, 128), F32
        ),
        scratch_shapes=[
            pltpu.VMEM((shots * offsets, samples), F32),
            pltpu.VMEM(table.shape, F32),
            pltpu.VMEM((samples // wide, wide, 128), F32),
            pltpu.SemaphoreType.DMA((shots,)),
            pltpu.SemaphoreType.DMA,
        ],
        compiler_params=pltpu.CompilerParams(vmem_limit_bytes=32 << 20),
        name="trace_blocks",
    )(*(pltpu.with_memory_space_constraint(a, pltpu.HBM) for a in (traces, table)))


def hold_kernel(x_ref, out_ref):
    pass


def hold(x):
    return pl.pallas_call(
        hold_kernel,
        in_specs=[pl.BlockSpec(memory_space=pl.ANY)],
        out_specs=pl.BlockSpec(memory_space=pl.ANY),
        out_shape=jax.ShapeDtypeStruct(x.shape, x.dtype),
        input_output_aliases={0: 0},
        compiler_params=pltpu.CompilerParams(vmem_limit_bytes=1 << 20),
        cost_estimate=pl.CostEstimate(flops=2 * 10**10, bytes_accessed=100 << 20, transcendentals=0),
        name="hold",
    )(x)


def gram_kernel(values_ref, source_ref, out_ref, acc_ref):
    step = pl.program_id(0)
    depth = values_ref.shape[0] * values_ref.shape[1]
    turned = values_ref[...].reshape(depth, 128).T
    pair = split(turned)
    source = source_ref[...]
    source = source.reshape(source.shape[0] // 2, 2, *source.shape[1:])
    acc = None
    for shot in range(2):
        rows = slice(64 * shot, 64 * shot + 64)
        weights = split(source[:, shot].reshape(depth, source.shape[3]))
        term = mm3((pair[0][rows], pair[1][rows]), weights, NN)
        acc = term if acc is None else acc + term

    @pl.when(step == 0)
    def _():
        acc_ref[...] = acc

    @pl.when(step > 0)
    def _():
        acc_ref[...] += acc

    @pl.when(step == pl.num_programs(0) - 1)
    def _():
        out_ref[...] = turn(acc_ref[...])


def turn(both):
    half, width = both.shape[0] // 2, both.shape[1] // 2
    real = both[:half, :width] - both[half:, width:]
    imag = both[half:, :width] + both[:half, width:]
    return jnp.concatenate([real, imag], axis=0)


def gram(values, sources):
    senders, box, lanes = values.shape
    shots, _, width = sources.shape
    steps = 2
    return pl.pallas_call(
        gram_kernel,
        grid=(steps,),
        in_specs=[
            pl.BlockSpec((senders // steps, box, lanes), lambda i: (i, 0, 0)),
            pl.BlockSpec((shots // steps, box, width), lambda i: (i, 0, 0)),
        ],
        out_specs=pl.BlockSpec((64, width // 2), lambda i: (0, 0)),
        out_shape=jax.ShapeDtypeStruct((64, width // 2), F32),
        scratch_shapes=[pltpu.VMEM((64, width), F32)],
        compiler_params=pltpu.CompilerParams(vmem_limit_bytes=32 << 20),
        name="gram",
    )(values, sources)


def own_kernel(c_ref, w_ref, own_ref, high_ref, low_ref):
    k = c_ref.shape[1]
    weights = w_ref[0]
    own = split(jnp.concatenate([weights[:, :k], weights[:, 2 * k : 3 * k]], axis=0))
    own_ref[...] = turn(mm3(split(c_ref[...]), own, NT))
    high, low = split(jnp.concatenate([weights[:, k : 2 * k], weights[:, 3 * k :]], axis=0))
    high_ref[...] = high
    low_ref[...] = low


def own_part(c, weights, level):
    rows, k = c.shape
    return pl.pallas_call(
        own_kernel,
        grid=(1,),
        in_specs=[
            pl.BlockSpec((rows, k), lambda i: (0, 0)),
            pl.BlockSpec((1, k, 4 * k), lambda i: (level, 0, 0)),
        ],
        out_specs=[
            pl.BlockSpec((rows, k), lambda i: (0, 0)),
            pl.BlockSpec((2 * k, k), lambda i: (0, 0)),
            pl.BlockSpec((2 * k, k), lambda i: (0, 0)),
        ],
        out_shape=[
            jax.ShapeDtypeStruct((rows, k), F32),
            jax.ShapeDtypeStruct((2 * k, k), BF16),
            jax.ShapeDtypeStruct((2 * k, k), BF16),
        ],
        compiler_params=pltpu.CompilerParams(vmem_limit_bytes=16 << 20),
        cost_estimate=pl.CostEstimate(flops=10**8, bytes_accessed=10**6, transcendentals=0),
        name="own_part",
    )(c, weights)


def joined(own_ref, c_ref, high_ref, low_ref):
    return own_ref[...] + turn(mm3(split(c_ref[...]), (high_ref[...], low_ref[...]), NT))


def join_kernel(own_ref, c_ref, high_ref, low_ref, out_ref):
    out_ref[...] = joined(own_ref, c_ref, high_ref, low_ref)


def last_kernel(own_ref, c_ref, high_ref, low_ref, e_ref, out_ref):
    c = joined(own_ref, c_ref, high_ref, low_ref)
    half = c.shape[0] // 2
    row = jnp.concatenate([c[:half], -c[half:]], axis=1)
    values = mm3(split(row), split(e_ref[...]), NT)
    for tile in range(values.shape[1] // 128):
        lanes = slice(128 * tile, 128 * tile + 128)
        parts = [values[8 * g : 8 * g + 8, lanes] for g in range(4)]
        for q, block in enumerate(move_groups(parts, 32)):
            out_ref[4 * tile + q] = block


def join_part(own, c, high, low):
    return pl.pallas_call(
        join_kernel,
        out_shape=jax.ShapeDtypeStruct(c.shape, F32),
        compiler_params=pltpu.CompilerParams(vmem_limit_bytes=16 << 20),
        name="join_part",
    )(own, c, high, low)


def last_part(own, c, high, low, e, freq_count):
    return pl.pallas_call(
        last_kernel,
        out_shape=jax.ShapeDtypeStruct((freq_count, 8, 128), F32),
        compiler_params=pltpu.CompilerParams(vmem_limit_bytes=16 << 20),
        name="last_part",
    )(own, c, high, low, e)


def final_kernel(x_ref, out_ref):
    x = x_ref[...].reshape(-1, 128)
    x = jnp.concatenate([x, jnp.zeros_like(x)], axis=0).T
    low = lax.broadcasted_iota(jnp.int32, (32, 128), 1) < 64
    for tile in range(2):
        first = x[64 * tile : 64 * tile + 32]
        second = x[64 * tile + 32 : 64 * tile + 64]
        out_ref[:, 128 * tile : 128 * tile + 128] = jnp.where(
            low, first, pltpu.roll(second, 64, 1)
        )


def final_part(x):
    return pl.pallas_call(
        final_kernel,
        out_shape=jax.ShapeDtypeStruct((32, TAUS), F32),
        compiler_params=pltpu.CompilerParams(vmem_limit_bytes=16 << 20),
        name="final_part",
    )(x)


def from_partner(block, axis, apart):
    count = lax.axis_size(axis)
    return lax.ppermute(block, axis, [(at, at ^ (1 << apart)) for at in range(count)])


def body(traces, source_weights, level_weights, slowness_weights):
    freq_count = lax.axis_size("freq")
    trace_count = lax.axis_size("trace")
    blocks = trace_blocks(traces, freq_count, trace_count)
    blocks = blocks.reshape(freq_count * trace_count, *blocks.shape[2:])
    blocks = hold(hold(blocks))
    values = lax.all_to_all(blocks, ("freq", "trace"), split_axis=0, concat_axis=0, tiled=True)
    c = gram(values, source_weights)
    levels = level_weights.shape[0]
    for level in range(levels):
        partner = from_partner(c, "trace", level)
        own, high, low = own_part(c, level_weights, level)
        if level < levels - 1:
            c = join_part(own, partner, high, low)
        else:
            out = last_part(own, partner, high, low, slowness_weights, freq_count)
    out = lax.all_to_all(out, "freq", split_axis=0, concat_axis=0, tiled=True)
    return final_part(out)


def solution(mesh):
    return jax.shard_map(
        body,
        mesh=mesh,
        in_specs=(
            P(("freq", "trace"), None, None),
            P(None, "trace", None),
            P(None, "trace", None),
            P("trace", None),
        ),
        out_specs=P(("trace", "freq"), None),
        check_vma=False,
    )
```

```python
import functools
import math

import jax
import jax.numpy as jnp
import numpy as np
from jax import lax
from jax.experimental import pallas as pl
from jax.experimental.pallas import tpu as pltpu
from jax.sharding import PartitionSpec as P

FREQS = 1024
TAUS = 256
F32 = jnp.float32
BF16 = jnp.bfloat16
NT = (((1,), (1,)), ((), ()))
NN = (((1,), (0,)), ((), ()))


def split(x):
    high = x.astype(BF16)
    return high, (x - high.astype(F32)).astype(BF16)


def mm(a, b, dims):
    return lax.dot_general(a, b, dims, preferred_element_type=F32)


def mm3(a_pair, b_pair, dims):
    rows = a_pair[0].shape[0]
    both = mm(jnp.concatenate(a_pair, axis=0), b_pair[0], dims)
    return both[:rows] + both[rows:] + mm(a_pair[0], b_pair[1], dims)


def lane_tau(lane):
    return 64 * (lane % 16 // 8) + 8 * (lane // 16) + lane % 8


def cot_table(samples, wide, scale):
    step = samples // (4 * TAUS)
    taus = lane_tau(np.arange(128))
    gap = wide * np.arange(samples // wide)[:, None, None] + step * taus
    gap = gap - (2 * np.arange(wide // 2)[None, :, None] + 1)
    return (scale / np.tan(np.pi * gap / samples)).astype(np.float32)


def move_groups(parts, width):
    count = len(parts)
    lanes = count * width
    group = lax.broadcasted_iota(jnp.int32, parts[0].shape, 1) // width
    turned = [p if x == 0 else pltpu.roll(p, width * x, 1) for x, p in enumerate(parts)]
    result = []
    for q in range(count):
        got = turned[(-q) % count]
        for spot in range(1, count):
            got = jnp.where(group == spot, turned[(spot - q) % count], got)
        result.append(got if q == 0 else pltpu.roll(got, lanes - width * q, 1))
    return result


def trace_kernel(scale, x_hbm, table_hbm, out_ref, x_ref, table_ref, full_ref, x_sem, table_sem):
    shots, offsets, samples = x_hbm.shape
    count, wide, _ = full_ref.shape
    rows = shots * offsets
    copies = [
        pltpu.make_async_copy(x_hbm.at[s], x_ref.at[pl.ds(s * offsets, offsets)], x_sem.at[s])
        for s in range(shots)
    ]
    table_copy = pltpu.make_async_copy(table_hbm, table_ref, table_sem)
    table_copy.start()
    for copy in copies:
        copy.start()
    lane = lax.broadcasted_iota(jnp.int32, (wide, 128), 1)
    row = lax.broadcasted_iota(jnp.int32, (wide, 128), 0)
    step = samples // (4 * TAUS)
    pick = jnp.where(row == step * lane_tau(lane), 1.0, 0.0).astype(BF16)
    full_ref[...] = jnp.zeros_like(full_ref)
    table_copy.wait()
    for d in range(count):
        full_ref[d, pl.ds(1, wide // 2, 2), :] = table_ref[d]
    table = [split(full_ref[d]) for d in range(count)]
    right = [
        jnp.concatenate(
            [
                jnp.concatenate([table[-at % count][part], table[(1 - at) % count][part]], axis=1)
                for at in range(count)
            ],
            axis=0,
        )
        for part in range(2)
    ]
    for copy in copies:
        copy.wait()
    x = x_ref[...]
    total = x[:, :128]
    for at in range(128, samples, 128):
        total = total + x[:, at : at + 128]
    pair = split(x)
    imag = mm3(pair, right, NN)
    odd = lax.broadcasted_iota(jnp.int32, total.shape, 1) % 2 == 1
    mean = jnp.sum(jnp.where(odd, total, 0.0), axis=1, keepdims=True) * scale
    real = []
    for half in range(2):
        part = slice(half * wide, half * wide + wide)
        both = mm(jnp.concatenate([p[:, part] for p in pair], axis=0), pick, NN)
        real.append((both[:rows] + both[rows:]) * (FREQS * scale) + mean)
    parts = []
    for s in range(shots):
        own = slice(s * offsets, s * offsets + offsets)
        parts += [real[0][own], real[1][own], imag[own, :128], imag[own, 128:]]
    for r, block in enumerate(move_groups(parts, 16)):
        out_ref[r] = block.reshape(out_ref.shape[1:])


def trace_blocks(traces, freq_count, trace_count):
    shots, offsets, samples = traces.shape
    wide = samples // 8
    scale = 1.0 / math.sqrt(samples) / math.sqrt(FREQS)
    table = jnp.asarray(cot_table(samples, wide, scale))
    return pl.pallas_call(
        functools.partial(trace_kernel, scale),
        in_specs=[pl.BlockSpec(memory_space=pltpu.HBM)] * 2,
        out_specs=pl.BlockSpec(memory_space=pltpu.VMEM),
        out_shape=jax.ShapeDtypeStruct(
            (freq_count, trace_count, offsets // trace_count, 128), F32
        ),
        scratch_shapes=[
            pltpu.VMEM((shots * offsets, samples), F32),
            pltpu.VMEM(table.shape, F32),
            pltpu.VMEM((samples // wide, wide, 128), F32),
            pltpu.SemaphoreType.DMA((shots,)),
            pltpu.SemaphoreType.DMA,
        ],
        compiler_params=pltpu.CompilerParams(vmem_limit_bytes=32 << 20),
        name="trace_blocks",
    )(*(pltpu.with_memory_space_constraint(a, pltpu.HBM) for a in (traces, table)))


def hold_kernel(x_ref, out_ref):
    pass


def hold(x):
    return pl.pallas_call(
        hold_kernel,
        in_specs=[pl.BlockSpec(memory_space=pl.ANY)],
        out_specs=pl.BlockSpec(memory_space=pl.ANY),
        out_shape=jax.ShapeDtypeStruct(x.shape, x.dtype),
        input_output_aliases={0: 0},
        compiler_params=pltpu.CompilerParams(vmem_limit_bytes=1 << 20),
        cost_estimate=pl.CostEstimate(flops=2 * 10**10, bytes_accessed=100 << 20, transcendentals=0),
        name="hold",
    )(x)


def gram_kernel(values_ref, source_ref, out_ref, acc_ref):
    step = pl.program_id(0)
    depth = values_ref.shape[0] * values_ref.shape[1]
    turned = values_ref[...].reshape(depth, 128).T
    pair = split(turned)
    source = source_ref[...]
    source = source.reshape(source.shape[0] // 2, 2, *source.shape[1:])
    acc = None
    for shot in range(2):
        rows = slice(64 * shot, 64 * shot + 64)
        weights = split(source[:, shot].reshape(depth, source.shape[3]))
        term = mm3((pair[0][rows], pair[1][rows]), weights, NN)
        acc = term if acc is None else acc + term

    @pl.when(step == 0)
    def _():
        acc_ref[...] = acc

    @pl.when(step > 0)
    def _():
        acc_ref[...] += acc

    @pl.when(step == pl.num_programs(0) - 1)
    def _():
        out_ref[...] = turn(acc_ref[...])


def turn(both):
    half, width = both.shape[0] // 2, both.shape[1] // 2
    real = both[:half, :width] - both[half:, width:]
    imag = both[half:, :width] + both[:half, width:]
    return jnp.concatenate([real, imag], axis=0)


def gram(values, sources):
    senders, box, lanes = values.shape
    shots, _, width = sources.shape
    steps = 2
    return pl.pallas_call(
        gram_kernel,
        grid=(steps,),
        in_specs=[
            pl.BlockSpec((senders // steps, box, lanes), lambda i: (i, 0, 0)),
            pl.BlockSpec((shots // steps, box, width), lambda i: (i, 0, 0)),
        ],
        out_specs=pl.BlockSpec((64, width // 2), lambda i: (0, 0)),
        out_shape=jax.ShapeDtypeStruct((64, width // 2), F32),
        scratch_shapes=[pltpu.VMEM((64, width), F32)],
        compiler_params=pltpu.CompilerParams(vmem_limit_bytes=32 << 20),
        name="gram",
    )(values, sources)


def fold(e, w, first):
    k = w.shape[0]
    left = split(jnp.concatenate([e[:, :k], e[:, k:]], axis=0))
    right = [w[:, at : at + k] for at in (first, first + 2 * k)]
    both = mm3(left, split(jnp.concatenate(right, axis=1)), NN)
    real = both[:k, :k] - both[k:, k:]
    imag = both[:k, k:] + both[k:, :k]
    return jnp.concatenate([real, imag], axis=1)


def far_kernel(e_ref, w_ref, after_ref, out_ref):
    out_ref[...] = fold(e_ref[...], w_ref[0], w_ref.shape[1])


def far_part(e, weights, after):
    levels, k, width = weights.shape
    return pl.pallas_call(
        far_kernel,
        grid=(1,),
        in_specs=[
            pl.BlockSpec(e.shape, lambda i: (0, 0)),
            pl.BlockSpec((1, k, width), lambda i: (levels - 1, 0, 0)),
            pl.BlockSpec(memory_space=pl.ANY),
        ],
        out_specs=pl.BlockSpec(e.shape, lambda i: (0, 0)),
        out_shape=jax.ShapeDtypeStruct(e.shape, F32),
        compiler_params=pltpu.CompilerParams(vmem_limit_bytes=16 << 20),
        cost_estimate=pl.CostEstimate(flops=5 * 10**8, bytes_accessed=10**6, transcendentals=0),
        name="far_part",
    )(e, weights, after)


def own_kernel(c_ref, w_ref, own_ref, high_ref, low_ref):
    k = c_ref.shape[1]
    weights = w_ref[0]
    own = split(jnp.concatenate([weights[:, :k], weights[:, 2 * k : 3 * k]], axis=0))
    own_ref[...] = turn(mm3(split(c_ref[...]), own, NT))
    high, low = split(jnp.concatenate([weights[:, k : 2 * k], weights[:, 3 * k :]], axis=0))
    high_ref[...] = high
    low_ref[...] = low


def own_fold_kernel(c_ref, w_ref, e_ref, last_ref, own_ref, high_ref, low_ref, *fold_refs):
    own_kernel(c_ref, w_ref, own_ref, high_ref, low_ref)
    for ref, part in zip(fold_refs, split(fold(e_ref[...], last_ref[0], 0))):
        ref[...] = part


def own_part(c, weights, level, e=None):
    rows, k = c.shape
    last = weights.shape[0] - 1
    whole = lambda *shape: pl.BlockSpec(shape, lambda i: (0,) * len(shape))
    sheet = lambda at: pl.BlockSpec((1, k, 4 * k), lambda i: (at, 0, 0))
    extra = () if e is None else (e, weights)
    pairs = [(2 * k, k)] * 2 + ([] if e is None else [e.shape] * 2)
    return pl.pallas_call(
        own_kernel if e is None else own_fold_kernel,
        grid=(1,),
        in_specs=[whole(rows, k), sheet(level)]
        + ([] if e is None else [whole(*e.shape), sheet(last)]),
        out_specs=[whole(rows, k)] + [whole(*p) for p in pairs],
        out_shape=[jax.ShapeDtypeStruct((rows, k), F32)]
        + [jax.ShapeDtypeStruct(p, BF16) for p in pairs],
        compiler_params=pltpu.CompilerParams(vmem_limit_bytes=16 << 20),
        cost_estimate=pl.CostEstimate(flops=10**8, bytes_accessed=10**6, transcendentals=0),
        name="own_part" if e is None else "own_fold_part",
    )(c, weights, *extra)


def joined(own_ref, c_ref, high_ref, low_ref):
    return own_ref[...] + turn(mm3(split(c_ref[...]), (high_ref[...], low_ref[...]), NT))


def join_kernel(own_ref, c_ref, high_ref, low_ref, out_ref):
    out_ref[...] = joined(own_ref, c_ref, high_ref, low_ref)


def last_kernel(own_ref, c_ref, high_ref, low_ref, near_high, near_low, far_ref, out_ref):
    c = joined(own_ref, c_ref, high_ref, low_ref)
    half = c.shape[0] // 2
    row = split(jnp.concatenate([c[:half], -c[half:]], axis=1))
    side = lax.axis_index("trace") // 8
    pairs = [(near_high[...], near_low[...]), split(far_ref[...])]
    for at, pair in enumerate(pairs):
        values = mm3(row, pair, NT)
        for tile in range(values.shape[1] // 128):
            lanes = slice(128 * tile, 128 * tile + 128)
            parts = [values[8 * g : 8 * g + 8, lanes] for g in range(4)]
            for q, block in enumerate(move_groups(parts, 32)):
                out_ref[2 * (4 * tile + q) + (at ^ side)] = block


def join_part(own, c, high, low):
    return pl.pallas_call(
        join_kernel,
        out_shape=jax.ShapeDtypeStruct(c.shape, F32),
        compiler_params=pltpu.CompilerParams(vmem_limit_bytes=16 << 20),
        name="join_part",
    )(own, c, high, low)


def last_part(own, c, high, low, near_high, near_low, far, freq_count):
    return pl.pallas_call(
        last_kernel,
        out_shape=jax.ShapeDtypeStruct((2 * freq_count, 8, 128), F32),
        compiler_params=pltpu.CompilerParams(vmem_limit_bytes=16 << 20),
        name="last_part",
    )(own, c, high, low, near_high, near_low, far)


def final_kernel(x_ref, out_ref):
    x = x_ref[...]
    x = x.reshape(x.shape[0] // 2, 2, 8, 128)
    x = (x[:, 0] + x[:, 1]).reshape(-1, 128)
    x = jnp.concatenate([x, jnp.zeros_like(x)], axis=0).T
    low = lax.broadcasted_iota(jnp.int32, (32, 128), 1) < 64
    for tile in range(2):
        first = x[64 * tile : 64 * tile + 32]
        second = x[64 * tile + 32 : 64 * tile + 64]
        out_ref[:, 128 * tile : 128 * tile + 128] = jnp.where(
            low, first, pltpu.roll(second, 64, 1)
        )


def final_part(x):
    return pl.pallas_call(
        final_kernel,
        out_shape=jax.ShapeDtypeStruct((32, TAUS), F32),
        compiler_params=pltpu.CompilerParams(vmem_limit_bytes=16 << 20),
        name="final_part",
    )(x)


def from_partner(block, axis, apart):
    count = lax.axis_size(axis)
    return lax.ppermute(block, axis, [(at, at ^ (1 << apart)) for at in range(count)])


def body(traces, source_weights, level_weights, slowness_weights):
    freq_count = lax.axis_size("freq")
    trace_count = lax.axis_size("trace")
    blocks = trace_blocks(traces, freq_count, trace_count)
    blocks = blocks.reshape(freq_count * trace_count, *blocks.shape[2:])
    blocks = hold(hold(blocks))
    values = lax.all_to_all(blocks, ("freq", "trace"), split_axis=0, concat_axis=0, tiled=True)
    last = level_weights.shape[0] - 1
    far = from_partner(far_part(slowness_weights, level_weights, values), "trace", last)
    c = gram(values, source_weights)
    for level in range(last):
        partner = from_partner(c, "trace", level)
        if level == 1:
            own, high, low, *near = own_part(c, level_weights, level, slowness_weights)
        else:
            own, high, low = own_part(c, level_weights, level)
        if level < last - 1:
            c = join_part(own, partner, high, low)
    out = last_part(own, partner, high, low, *near, far, freq_count)
    half = trace_count // 2
    groups = [
        [r * trace_count + t * half + rest for r in range(freq_count) for t in range(2)]
        for rest in range(half)
    ]
    out = lax.all_to_all(
        out, ("freq", "trace"), 0, 0, axis_index_groups=groups, tiled=True
    )
    return final_part(out)


def solution(mesh):
    return jax.shard_map(
        body,
        mesh=mesh,
        in_specs=(
            P(("freq", "trace"), None, None),
            P(None, "trace", None),
            P(None, "trace", None),
            P("trace", None),
        ),
        out_specs=P(("trace", "freq"), None),
        check_vma=False,
    )
```

```python
import functools
import math

import jax
import jax.numpy as jnp
import numpy as np
from jax import lax
from jax.experimental import pallas as pl
from jax.experimental.pallas import tpu as pltpu
from jax.sharding import PartitionSpec as P

FREQS = 1024
TAUS = 256
F32 = jnp.float32
BF16 = jnp.bfloat16
NT = (((1,), (1,)), ((), ()))
NN = (((1,), (0,)), ((), ()))


def split(x):
    high = x.astype(BF16)
    return high, (x - high.astype(F32)).astype(BF16)


def mm(a, b, dims):
    return lax.dot_general(a, b, dims, preferred_element_type=F32)


def mm3(a_pair, b_pair, dims):
    rows = a_pair[0].shape[0]
    both = mm(jnp.concatenate(a_pair, axis=0), b_pair[0], dims)
    return both[:rows] + both[rows:] + mm(a_pair[0], b_pair[1], dims)


def lane_tau(lane):
    return 64 * (lane % 16 // 8) + 8 * (lane // 16) + lane % 8


def cot_table(samples, wide, scale):
    step = samples // (4 * TAUS)
    taus = lane_tau(np.arange(128))
    gap = wide * np.arange(samples // wide)[:, None, None] + step * taus
    gap = gap - (2 * np.arange(wide // 2)[None, :, None] + 1)
    return (scale / np.tan(np.pi * gap / samples)).astype(np.float32)


def move_groups(parts, width):
    count = len(parts)
    lanes = count * width
    group = lax.broadcasted_iota(jnp.int32, parts[0].shape, 1) // width
    turned = [p if x == 0 else pltpu.roll(p, width * x, 1) for x, p in enumerate(parts)]
    result = []
    for q in range(count):
        got = turned[(-q) % count]
        for spot in range(1, count):
            got = jnp.where(group == spot, turned[(spot - q) % count], got)
        result.append(got if q == 0 else pltpu.roll(got, lanes - width * q, 1))
    return result


def trace_kernel(scale, x_hbm, table_hbm, out_ref, x_ref, table_ref, high_ref, low_ref, x_sem, table_sem):
    shots, offsets, samples = x_hbm.shape
    count, wide, _ = high_ref.shape
    rows = shots * offsets
    copies = [
        pltpu.make_async_copy(x_hbm.at[s], x_ref.at[pl.ds(s * offsets, offsets)], x_sem.at[s])
        for s in range(shots)
    ]
    table_copy = pltpu.make_async_copy(table_hbm, table_ref, table_sem)
    table_copy.start()
    for copy in copies:
        copy.start()
    lane = lax.broadcasted_iota(jnp.int32, (wide, 128), 1)
    row = lax.broadcasted_iota(jnp.int32, (wide, 128), 0)
    pick = jnp.where(row // 2 == lane_tau(lane), 1.0, 0.0).astype(BF16)
    table_copy.wait()
    even_rows, odd_rows = pl.ds(0, wide // 2, 2), pl.ds(1, wide // 2, 2)
    for d in range(count):
        table = table_ref[d]
        high = table.astype(BF16).astype(F32)
        high_ref[d, even_rows, :] = high
        high_ref[d, odd_rows, :] = high
        low_ref[d, odd_rows, :] = table - high
        low_ref[(d + count // 2) % count, even_rows, :] = table - high

    def right(ref, blocks):
        part = [ref[d].astype(BF16) for d in range(count)]
        return jnp.concatenate(
            [
                jnp.concatenate([part[-at % count], part[(1 - at) % count]], axis=1)
                for at in range(blocks)
            ],
            axis=0,
        )

    high_table, low_table = right(high_ref, count), right(low_ref, count // 2)
    for copy in copies:
        copy.wait()
    tiles = range(0, samples, 128)
    odd = lax.broadcasted_iota(jnp.int32, (rows, 128), 1) % 2 == 1
    total, high, low = None, [], []
    for at in tiles:
        x = x_ref[:, at : at + 128]
        total = x if total is None else total + x
        pair = split(x)
        high.append(pair[0])
        low.append(pair[1])
    mix = lambda on_odd, on_even, by: jnp.concatenate(
        [jnp.where(odd, o, pltpu.roll(e, by, 1)) for o, e in zip(on_odd, on_even)], axis=1
    )
    middle = len(high) // 2
    imag = mm(mix(high, low, 127), high_table, NN) + mm(
        mix(high[:middle], high[middle:], 127), low_table, NN
    )
    mean = jnp.sum(jnp.where(odd, total, 0.0), axis=1, keepdims=True) * scale
    real = []
    for at in range(2):
        part = slice(at * wide // 128, (at + 1) * wide // 128)
        both = [jnp.where(odd, pltpu.roll(e, 1, 1), o) for o, e in zip(high[part], low[part])]
        real.append(mm(jnp.concatenate(both, axis=1), pick, NN) * (FREQS * scale) + mean)
    parts = []
    for s in range(shots):
        own = slice(s * offsets, s * offsets + offsets)
        parts += [real[0][own], real[1][own], imag[own, :128], imag[own, 128:]]
    for r, block in enumerate(move_groups(parts, 16)):
        out_ref[r] = block.reshape(out_ref.shape[1:])


def trace_blocks(traces, freq_count, trace_count):
    shots, offsets, samples = traces.shape
    wide = samples // 8
    scale = 1.0 / math.sqrt(samples) / math.sqrt(FREQS)
    table = jnp.asarray(cot_table(samples, wide, scale))
    return pl.pallas_call(
        functools.partial(trace_kernel, scale),
        in_specs=[pl.BlockSpec(memory_space=pltpu.HBM)] * 2,
        out_specs=pl.BlockSpec(memory_space=pltpu.VMEM),
        out_shape=jax.ShapeDtypeStruct(
            (freq_count, trace_count, offsets // trace_count, 128), F32
        ),
        scratch_shapes=[
            pltpu.VMEM((shots * offsets, samples), F32),
            pltpu.VMEM(table.shape, F32),
            pltpu.VMEM((samples // wide, wide, 128), F32),
            pltpu.VMEM((samples // wide, wide, 128), F32),
            pltpu.SemaphoreType.DMA((shots,)),
            pltpu.SemaphoreType.DMA,
        ],
        compiler_params=pltpu.CompilerParams(vmem_limit_bytes=32 << 20),
        name="trace_blocks",
    )(*(pltpu.with_memory_space_constraint(a, pltpu.HBM) for a in (traces, table)))


def hold_kernel(x_ref, out_ref):
    pass


def hold(x):
    return pl.pallas_call(
        hold_kernel,
        in_specs=[pl.BlockSpec(memory_space=pl.ANY)],
        out_specs=pl.BlockSpec(memory_space=pl.ANY),
        out_shape=jax.ShapeDtypeStruct(x.shape, x.dtype),
        input_output_aliases={0: 0},
        compiler_params=pltpu.CompilerParams(vmem_limit_bytes=1 << 20),
        cost_estimate=pl.CostEstimate(flops=2 * 10**10, bytes_accessed=100 << 20, transcendentals=0),
        name="hold",
    )(x)


def gram_kernel(values_ref, source_ref, out_ref, acc_ref):
    step = pl.program_id(0)
    depth = values_ref.shape[0] * values_ref.shape[1]
    turned = values_ref[...].reshape(depth, 128).T
    pair = split(turned)
    source = source_ref[...]
    source = source.reshape(source.shape[0] // 2, 2, *source.shape[1:])
    acc = None
    for shot in range(2):
        rows = slice(64 * shot, 64 * shot + 64)
        weights = split(source[:, shot].reshape(depth, source.shape[3]))
        term = mm3((pair[0][rows], pair[1][rows]), weights, NN)
        acc = term if acc is None else acc + term

    @pl.when(step == 0)
    def _():
        acc_ref[...] = acc

    @pl.when(step > 0)
    def _():
        acc_ref[...] += acc

    @pl.when(step == pl.num_programs(0) - 1)
    def _():
        out_ref[...] = turn(acc_ref[...])


def turn(both):
    half, width = both.shape[0] // 2, both.shape[1] // 2
    real = both[:half, :width] - both[half:, width:]
    imag = both[half:, :width] + both[:half, width:]
    return jnp.concatenate([real, imag], axis=0)


def gram(values, sources):
    senders, box, lanes = values.shape
    shots, _, width = sources.shape
    steps = 1
    return pl.pallas_call(
        gram_kernel,
        grid=(steps,),
        in_specs=[
            pl.BlockSpec((senders // steps, box, lanes), lambda i: (i, 0, 0)),
            pl.BlockSpec((shots // steps, box, width), lambda i: (i, 0, 0)),
        ],
        out_specs=pl.BlockSpec((64, width // 2), lambda i: (0, 0)),
        out_shape=jax.ShapeDtypeStruct((64, width // 2), F32),
        scratch_shapes=[pltpu.VMEM((64, width), F32)],
        compiler_params=pltpu.CompilerParams(vmem_limit_bytes=32 << 20),
        name="gram",
    )(values, sources)


def fold(e, w, first):
    k = w.shape[0]
    left = split(jnp.concatenate([e[:, :k], e[:, k:]], axis=0))
    right = [w[:, at : at + k] for at in (first, first + 2 * k)]
    both = mm3(left, split(jnp.concatenate(right, axis=1)), NN)
    real = both[:k, :k] - both[k:, k:]
    imag = both[:k, k:] + both[k:, :k]
    return jnp.concatenate([real, imag], axis=1)


def far_kernel(e_ref, w_ref, after_ref, out_ref):
    out_ref[...] = fold(e_ref[...], w_ref[0], w_ref.shape[1])


def far_part(e, weights, after):
    levels, k, width = weights.shape
    return pl.pallas_call(
        far_kernel,
        grid=(1,),
        in_specs=[
            pl.BlockSpec(e.shape, lambda i: (0, 0)),
            pl.BlockSpec((1, k, width), lambda i: (levels - 1, 0, 0)),
            pl.BlockSpec(memory_space=pl.ANY),
        ],
        out_specs=pl.BlockSpec(e.shape, lambda i: (0, 0)),
        out_shape=jax.ShapeDtypeStruct(e.shape, F32),
        compiler_params=pltpu.CompilerParams(vmem_limit_bytes=16 << 20),
        cost_estimate=pl.CostEstimate(flops=5 * 10**8, bytes_accessed=10**6, transcendentals=0),
        name="far_part",
    )(e, weights, after)


def own_kernel(c_ref, w_ref, own_ref, high_ref, low_ref):
    k = c_ref.shape[1]
    weights = w_ref[0]
    own = split(jnp.concatenate([weights[:, :k], weights[:, 2 * k : 3 * k]], axis=0))
    own_ref[...] = turn(mm3(split(c_ref[...]), own, NT))
    high, low = split(jnp.concatenate([weights[:, k : 2 * k], weights[:, 3 * k :]], axis=0))
    high_ref[...] = high
    low_ref[...] = low


def own_fold_kernel(c_ref, w_ref, e_ref, last_ref, own_ref, high_ref, low_ref, *fold_refs):
    own_kernel(c_ref, w_ref, own_ref, high_ref, low_ref)
    for ref, part in zip(fold_refs, split(fold(e_ref[...], last_ref[0], 0))):
        ref[...] = part


def own_part(c, weights, level, e=None):
    rows, k = c.shape
    last = weights.shape[0] - 1
    whole = lambda *shape: pl.BlockSpec(shape, lambda i: (0,) * len(shape))
    sheet = lambda at: pl.BlockSpec((1, k, 4 * k), lambda i: (at, 0, 0))
    extra = () if e is None else (e, weights)
    pairs = [(2 * k, k)] * 2 + ([] if e is None else [e.shape] * 2)
    return pl.pallas_call(
        own_kernel if e is None else own_fold_kernel,
        grid=(1,),
        in_specs=[whole(rows, k), sheet(level)]
        + ([] if e is None else [whole(*e.shape), sheet(last)]),
        out_specs=[whole(rows, k)] + [whole(*p) for p in pairs],
        out_shape=[jax.ShapeDtypeStruct((rows, k), F32)]
        + [jax.ShapeDtypeStruct(p, BF16) for p in pairs],
        compiler_params=pltpu.CompilerParams(vmem_limit_bytes=16 << 20),
        cost_estimate=pl.CostEstimate(flops=10**8, bytes_accessed=10**6, transcendentals=0),
        name="own_part" if e is None else "own_fold_part",
    )(c, weights, *extra)


def joined(own_ref, c_ref, high_ref, low_ref):
    return own_ref[...] + turn(mm3(split(c_ref[...]), (high_ref[...], low_ref[...]), NT))


def join_kernel(own_ref, c_ref, high_ref, low_ref, out_ref):
    out_ref[...] = joined(own_ref, c_ref, high_ref, low_ref)


def last_kernel(own_ref, c_ref, high_ref, low_ref, near_high, near_low, far_ref, out_ref):
    c = joined(own_ref, c_ref, high_ref, low_ref)
    half = c.shape[0] // 2
    row = split(jnp.concatenate([c[:half], -c[half:]], axis=1))
    side = lax.axis_index("trace") // 8
    pairs = [(near_high[...], near_low[...]), split(far_ref[...])]
    for at, pair in enumerate(pairs):
        values = mm3(row, pair, NT)
        for tile in range(values.shape[1] // 128):
            lanes = slice(128 * tile, 128 * tile + 128)
            parts = [values[8 * g : 8 * g + 8, lanes] for g in range(4)]
            for q, block in enumerate(move_groups(parts, 32)):
                out_ref[2 * (4 * tile + q) + (at ^ side)] = block


def join_part(own, c, high, low):
    return pl.pallas_call(
        join_kernel,
        out_shape=jax.ShapeDtypeStruct(c.shape, F32),
        compiler_params=pltpu.CompilerParams(vmem_limit_bytes=16 << 20),
        name="join_part",
    )(own, c, high, low)


def last_part(own, c, high, low, near_high, near_low, far, freq_count):
    return pl.pallas_call(
        last_kernel,
        out_shape=jax.ShapeDtypeStruct((2 * freq_count, 8, 128), F32),
        compiler_params=pltpu.CompilerParams(vmem_limit_bytes=16 << 20),
        name="last_part",
    )(own, c, high, low, near_high, near_low, far)


def final_kernel(x_ref, out_ref):
    x = x_ref[...]
    x = x.reshape(x.shape[0] // 2, 2, 8, 128)
    x = (x[:, 0] + x[:, 1]).reshape(-1, 128)
    x = jnp.concatenate([x, jnp.zeros_like(x)], axis=0).T
    low = lax.broadcasted_iota(jnp.int32, (32, 128), 1) < 64
    for tile in range(2):
        first = x[64 * tile : 64 * tile + 32]
        second = x[64 * tile + 32 : 64 * tile + 64]
        out_ref[:, 128 * tile : 128 * tile + 128] = jnp.where(
            low, first, pltpu.roll(second, 64, 1)
        )


def final_part(x):
    return pl.pallas_call(
        final_kernel,
        out_shape=jax.ShapeDtypeStruct((32, TAUS), F32),
        compiler_params=pltpu.CompilerParams(vmem_limit_bytes=16 << 20),
        name="final_part",
    )(x)


def from_partner(block, axis, apart):
    count = lax.axis_size(axis)
    return lax.ppermute(block, axis, [(at, at ^ (1 << apart)) for at in range(count)])


def body(traces, source_weights, level_weights, slowness_weights):
    freq_count = lax.axis_size("freq")
    trace_count = lax.axis_size("trace")
    blocks = trace_blocks(traces, freq_count, trace_count)
    blocks = blocks.reshape(freq_count * trace_count, *blocks.shape[2:])
    blocks = hold(hold(blocks))
    values = lax.all_to_all(blocks, ("freq", "trace"), split_axis=0, concat_axis=0, tiled=True)
    last = level_weights.shape[0] - 1
    far = from_partner(far_part(slowness_weights, level_weights, values), "trace", last)
    c = gram(values, source_weights)
    for level in range(last):
        partner = from_partner(c, "trace", level)
        if level == 1:
            own, high, low, *near = own_part(c, level_weights, level, slowness_weights)
        else:
            own, high, low = own_part(c, level_weights, level)
        if level < last - 1:
            c = join_part(own, partner, high, low)
    out = last_part(own, partner, high, low, *near, far, freq_count)
    half = trace_count // 2
    groups = [
        [r * trace_count + t * half + rest for r in range(freq_count) for t in range(2)]
        for rest in range(half)
    ]
    out = lax.all_to_all(
        out, ("freq", "trace"), 0, 0, axis_index_groups=groups, tiled=True
    )
    return final_part(out)


def solution(mesh):
    return jax.shard_map(
        body,
        mesh=mesh,
        in_specs=(
            P(("freq", "trace"), None, None),
            P(None, "trace", None),
            P(None, "trace", None),
            P("trace", None),
        ),
        out_specs=P(("trace", "freq"), None),
        check_vma=False,
    )
```

```python
import functools
import math

import jax
import jax.numpy as jnp
import numpy as np
from jax import lax
from jax.experimental import pallas as pl
from jax.experimental.pallas import tpu as pltpu
from jax.sharding import PartitionSpec as P

FREQS = 1024
TAUS = 256
F32 = jnp.float32
BF16 = jnp.bfloat16
NT = (((1,), (1,)), ((), ()))
NN = (((1,), (0,)), ((), ()))


def split(x):
    high = x.astype(BF16)
    return high, (x - high.astype(F32)).astype(BF16)


def mm(a, b, dims):
    return lax.dot_general(a, b, dims, preferred_element_type=F32)


def mm3(a_pair, b_pair, dims):
    rows = a_pair[0].shape[0]
    both = mm(jnp.concatenate(a_pair, axis=0), b_pair[0], dims)
    return both[:rows] + both[rows:] + mm(a_pair[0], b_pair[1], dims)


def lane_tau(lane):
    return 64 * (lane % 16 // 8) + 8 * (lane // 16) + lane % 8


def cot_table(samples, wide, scale):
    step = samples // (4 * TAUS)
    taus = lane_tau(np.arange(128))
    gap = wide * np.arange(samples // wide)[:, None, None] + step * taus
    gap = gap - (2 * np.arange(wide // 2)[None, :, None] + 1)
    return (scale / np.tan(np.pi * gap / samples)).astype(np.float32)


def move_groups(parts, width):
    count = len(parts)
    lanes = count * width
    group = lax.broadcasted_iota(jnp.int32, parts[0].shape, 1) // width
    turned = [p if x == 0 else pltpu.roll(p, width * x, 1) for x, p in enumerate(parts)]
    result = []
    for q in range(count):
        got = turned[(-q) % count]
        for spot in range(1, count):
            got = jnp.where(group == spot, turned[(spot - q) % count], got)
        result.append(got if q == 0 else pltpu.roll(got, lanes - width * q, 1))
    return result


def trace_kernel(scale, x_hbm, table_hbm, out_ref, x_ref, table_ref, high_ref, low_ref, x_sem, table_sem):
    shots, offsets, samples = x_hbm.shape
    count, wide, _ = high_ref.shape
    rows = shots * offsets
    copies = [
        pltpu.make_async_copy(x_hbm.at[s], x_ref.at[pl.ds(s * offsets, offsets)], x_sem.at[s])
        for s in range(shots)
    ]
    table_copy = pltpu.make_async_copy(table_hbm, table_ref, table_sem)
    table_copy.start()
    for copy in copies:
        copy.start()
    lane = lax.broadcasted_iota(jnp.int32, (wide, 128), 1)
    row = lax.broadcasted_iota(jnp.int32, (wide, 128), 0)
    pick = jnp.where(row // 2 == lane_tau(lane), 1.0, 0.0).astype(BF16)
    table_copy.wait()
    even_rows, odd_rows = pl.ds(0, wide // 2, 2), pl.ds(1, wide // 2, 2)
    for d in range(count):
        table = table_ref[d]
        high = table.astype(BF16).astype(F32)
        high_ref[d, even_rows, :] = high
        high_ref[d, odd_rows, :] = high
        low_ref[d, odd_rows, :] = table - high
        low_ref[(d + count // 2) % count, even_rows, :] = table - high

    def right(ref, blocks):
        part = [ref[d].astype(BF16) for d in range(count)]
        return jnp.concatenate(
            [
                jnp.concatenate([part[-at % count], part[(1 - at) % count]], axis=1)
                for at in range(blocks)
            ],
            axis=0,
        )

    high_table, low_table = right(high_ref, count), right(low_ref, count // 2)
    for copy in copies:
        copy.wait()
    tiles = range(0, samples, 128)
    odd = lax.broadcasted_iota(jnp.int32, (rows, 128), 1) % 2 == 1
    total, high, low = None, [], []
    for at in tiles:
        x = x_ref[:, at : at + 128]
        total = x if total is None else total + x
        pair = split(x)
        high.append(pair[0])
        low.append(pair[1])
    mix = lambda on_odd, on_even, by: jnp.concatenate(
        [jnp.where(odd, o, pltpu.roll(e, by, 1)) for o, e in zip(on_odd, on_even)], axis=1
    )
    middle = len(high) // 2
    imag = mm(mix(high, low, 127), high_table, NN) + mm(
        mix(high[:middle], high[middle:], 127), low_table, NN
    )
    mean = jnp.sum(jnp.where(odd, total, 0.0), axis=1, keepdims=True) * scale
    real = []
    for at in range(2):
        part = slice(at * wide // 128, (at + 1) * wide // 128)
        both = [jnp.where(odd, pltpu.roll(e, 1, 1), o) for o, e in zip(high[part], low[part])]
        real.append(mm(jnp.concatenate(both, axis=1), pick, NN) * (FREQS * scale) + mean)
    parts = []
    for s in range(shots):
        own = slice(s * offsets, s * offsets + offsets)
        parts += [real[0][own], real[1][own], imag[own, :128], imag[own, 128:]]
    for r, block in enumerate(move_groups(parts, 16)):
        out_ref[r] = block.reshape(out_ref.shape[1:])


def trace_blocks(traces, freq_count, trace_count):
    shots, offsets, samples = traces.shape
    wide = samples // 8
    scale = 1.0 / math.sqrt(samples) / math.sqrt(FREQS)
    table = jnp.asarray(cot_table(samples, wide, scale))
    return pl.pallas_call(
        functools.partial(trace_kernel, scale),
        in_specs=[pl.BlockSpec(memory_space=pltpu.HBM)] * 2,
        out_specs=pl.BlockSpec(memory_space=pltpu.VMEM),
        out_shape=jax.ShapeDtypeStruct(
            (freq_count, trace_count, offsets // trace_count, 128), F32
        ),
        scratch_shapes=[
            pltpu.VMEM((shots * offsets, samples), F32),
            pltpu.VMEM(table.shape, F32),
            pltpu.VMEM((samples // wide, wide, 128), F32),
            pltpu.VMEM((samples // wide, wide, 128), F32),
            pltpu.SemaphoreType.DMA((shots,)),
            pltpu.SemaphoreType.DMA,
        ],
        compiler_params=pltpu.CompilerParams(vmem_limit_bytes=32 << 20),
        name="trace_blocks",
    )(*(pltpu.with_memory_space_constraint(a, pltpu.HBM) for a in (traces, table)))


def hold_kernel(x_ref, out_ref):
    pass


def hold(x):
    return pl.pallas_call(
        hold_kernel,
        in_specs=[pl.BlockSpec(memory_space=pl.ANY)],
        out_specs=pl.BlockSpec(memory_space=pl.ANY),
        out_shape=jax.ShapeDtypeStruct(x.shape, x.dtype),
        input_output_aliases={0: 0},
        compiler_params=pltpu.CompilerParams(vmem_limit_bytes=1 << 20),
        cost_estimate=pl.CostEstimate(flops=2 * 10**10, bytes_accessed=100 << 20, transcendentals=0),
        name="hold",
    )(x)


def gram_kernel(values_ref, source_ref, out_ref, acc_ref):
    step = pl.program_id(0)
    depth = values_ref.shape[0] * values_ref.shape[1]
    turned = values_ref[...].reshape(depth, 128).T
    pair = split(turned)
    source = source_ref[...]
    source = source.reshape(source.shape[0] // 2, 2, *source.shape[1:])
    acc = None
    for shot in range(2):
        rows = slice(64 * shot, 64 * shot + 64)
        weights = split(source[:, shot].reshape(depth, source.shape[3]))
        term = mm3((pair[0][rows], pair[1][rows]), weights, NN)
        acc = term if acc is None else acc + term

    @pl.when(step == 0)
    def _():
        acc_ref[...] = acc

    @pl.when(step > 0)
    def _():
        acc_ref[...] += acc

    @pl.when(step == pl.num_programs(0) - 1)
    def _():
        out_ref[...] = turn(acc_ref[...])


def turn(both):
    half, width = both.shape[0] // 2, both.shape[1] // 2
    real = both[:half, :width] - both[half:, width:]
    imag = both[half:, :width] + both[:half, width:]
    return jnp.concatenate([real, imag], axis=0)


def gram(values, sources):
    senders, box, lanes = values.shape
    shots, _, width = sources.shape
    steps = 1
    return pl.pallas_call(
        gram_kernel,
        grid=(steps,),
        in_specs=[
            pl.BlockSpec((senders // steps, box, lanes), lambda i: (i, 0, 0)),
            pl.BlockSpec((shots // steps, box, width), lambda i: (i, 0, 0)),
        ],
        out_specs=pl.BlockSpec((64, width // 2), lambda i: (0, 0)),
        out_shape=jax.ShapeDtypeStruct((64, width // 2), F32),
        scratch_shapes=[pltpu.VMEM((64, width), F32)],
        compiler_params=pltpu.CompilerParams(vmem_limit_bytes=32 << 20),
        name="gram",
    )(values, sources)


def fold(e, w, first):
    k = w.shape[0]
    left = split(jnp.concatenate([e[:, :k], e[:, k:]], axis=0))
    right = [w[:, at : at + k] for at in (first, first + 2 * k)]
    both = mm3(left, split(jnp.concatenate(right, axis=1)), NN)
    real = both[:k, :k] - both[k:, k:]
    imag = both[:k, k:] + both[k:, :k]
    return jnp.concatenate([real, imag], axis=1)


def far_kernel(e_ref, w_ref, after_ref, out_ref):
    out_ref[...] = fold(e_ref[...], w_ref[0], w_ref.shape[1])


def far_part(e, weights, after):
    levels, k, width = weights.shape
    return pl.pallas_call(
        far_kernel,
        grid=(1,),
        in_specs=[
            pl.BlockSpec(e.shape, lambda i: (0, 0)),
            pl.BlockSpec((1, k, width), lambda i: (levels - 1, 0, 0)),
            pl.BlockSpec(memory_space=pl.ANY),
        ],
        out_specs=pl.BlockSpec(e.shape, lambda i: (0, 0)),
        out_shape=jax.ShapeDtypeStruct(e.shape, F32),
        compiler_params=pltpu.CompilerParams(vmem_limit_bytes=16 << 20),
        cost_estimate=pl.CostEstimate(flops=5 * 10**8, bytes_accessed=10**6, transcendentals=0),
        name="far_part",
    )(e, weights, after)


def own_kernel(c_ref, w_ref, own_ref, high_ref, low_ref):
    k = c_ref.shape[1]
    weights = w_ref[0]
    own = split(jnp.concatenate([weights[:, :k], weights[:, 2 * k : 3 * k]], axis=0))
    own_ref[...] = turn(mm3(split(c_ref[...]), own, NT))
    partner = jnp.concatenate([weights[:, k : 2 * k], weights[:, 3 * k :]], axis=0)
    high, low = split(partner.T)
    high_ref[...] = high
    low_ref[...] = low


def own_fold_kernel(c_ref, w_ref, e_ref, last_ref, own_ref, high_ref, low_ref, *fold_refs):
    own_kernel(c_ref, w_ref, own_ref, high_ref, low_ref)
    for ref, part in zip(fold_refs, split(fold(e_ref[...], last_ref[0], 0).T)):
        ref[...] = part


def own_part(c, weights, level, e=None):
    rows, k = c.shape
    last = weights.shape[0] - 1
    whole = lambda *shape: pl.BlockSpec(shape, lambda i: (0,) * len(shape))
    sheet = lambda at: pl.BlockSpec((1, k, 4 * k), lambda i: (at, 0, 0))
    extra = () if e is None else (e, weights)
    pairs = [(k, 2 * k)] * 2 + ([] if e is None else [e.shape[::-1]] * 2)
    return pl.pallas_call(
        own_kernel if e is None else own_fold_kernel,
        grid=(1,),
        in_specs=[whole(rows, k), sheet(level)]
        + ([] if e is None else [whole(*e.shape), sheet(last)]),
        out_specs=[whole(rows, k)] + [whole(*p) for p in pairs],
        out_shape=[jax.ShapeDtypeStruct((rows, k), F32)]
        + [jax.ShapeDtypeStruct(p, BF16) for p in pairs],
        compiler_params=pltpu.CompilerParams(vmem_limit_bytes=16 << 20),
        cost_estimate=pl.CostEstimate(flops=10**8, bytes_accessed=10**6, transcendentals=0),
        name="own_part" if e is None else "own_fold_part",
    )(c, weights, *extra)


def joined(own_ref, c_ref, high_ref, low_ref):
    return own_ref[...] + turn(mm3(split(c_ref[...]), (high_ref[...], low_ref[...]), NN))


def join_kernel(own_ref, c_ref, high_ref, low_ref, out_ref):
    out_ref[...] = joined(own_ref, c_ref, high_ref, low_ref)


def last_kernel(own_ref, c_ref, high_ref, low_ref, near_high, near_low, far_ref, out_ref):
    c = joined(own_ref, c_ref, high_ref, low_ref)
    half = c.shape[0] // 2
    row = split(jnp.concatenate([c[:half], -c[half:]], axis=1))
    side = lax.axis_index("trace") // 8
    pairs = [(near_high[...], near_low[...]), split(far_ref[...])]
    for at, pair in enumerate(pairs):
        values = mm3(row, pair, NT if at else NN)
        for tile in range(values.shape[1] // 128):
            lanes = slice(128 * tile, 128 * tile + 128)
            parts = [values[8 * g : 8 * g + 8, lanes] for g in range(4)]
            for q, block in enumerate(move_groups(parts, 32)):
                out_ref[2 * (4 * tile + q) + (at ^ side)] = block


def join_part(own, c, high, low):
    return pl.pallas_call(
        join_kernel,
        out_shape=jax.ShapeDtypeStruct(c.shape, F32),
        compiler_params=pltpu.CompilerParams(vmem_limit_bytes=16 << 20),
        name="join_part",
    )(own, c, high, low)


def last_part(own, c, high, low, near_high, near_low, far, freq_count):
    return pl.pallas_call(
        last_kernel,
        out_shape=jax.ShapeDtypeStruct((2 * freq_count, 8, 128), F32),
        compiler_params=pltpu.CompilerParams(vmem_limit_bytes=16 << 20),
        name="last_part",
    )(own, c, high, low, near_high, near_low, far)


def final_kernel(x_ref, out_ref):
    x = x_ref[...]
    x = x.reshape(x.shape[0] // 2, 2, 8, 128)
    x = (x[:, 0] + x[:, 1]).reshape(-1, 128)
    x = jnp.concatenate([x, jnp.zeros_like(x)], axis=0).T
    low = lax.broadcasted_iota(jnp.int32, (32, 128), 1) < 64
    for tile in range(2):
        first = x[64 * tile : 64 * tile + 32]
        second = x[64 * tile + 32 : 64 * tile + 64]
        out_ref[:, 128 * tile : 128 * tile + 128] = jnp.where(
            low, first, pltpu.roll(second, 64, 1)
        )


def final_part(x):
    return pl.pallas_call(
        final_kernel,
        out_shape=jax.ShapeDtypeStruct((32, TAUS), F32),
        compiler_params=pltpu.CompilerParams(vmem_limit_bytes=16 << 20),
        name="final_part",
    )(x)


def from_partner(block, axis, apart):
    count = lax.axis_size(axis)
    return lax.ppermute(block, axis, [(at, at ^ (1 << apart)) for at in range(count)])


def body(traces, source_weights, level_weights, slowness_weights):
    freq_count = lax.axis_size("freq")
    trace_count = lax.axis_size("trace")
    blocks = trace_blocks(traces, freq_count, trace_count)
    blocks = blocks.reshape(freq_count * trace_count, *blocks.shape[2:])
    blocks = hold(hold(blocks))
    values = lax.all_to_all(blocks, ("freq", "trace"), split_axis=0, concat_axis=0, tiled=True)
    last = level_weights.shape[0] - 1
    far = from_partner(far_part(slowness_weights, level_weights, values), "trace", last)
    c = gram(values, source_weights)
    for level in range(last):
        partner = from_partner(c, "trace", level)
        if level == 1:
            own, high, low, *near = own_part(c, level_weights, level, slowness_weights)
        else:
            own, high, low = own_part(c, level_weights, level)
        if level < last - 1:
            c = join_part(own, partner, high, low)
    out = last_part(own, partner, high, low, *near, far, freq_count)
    half = trace_count // 2
    groups = [
        [r * trace_count + t * half + rest for r in range(freq_count) for t in range(2)]
        for rest in range(half)
    ]
    out = lax.all_to_all(
        out, ("freq", "trace"), 0, 0, axis_index_groups=groups, tiled=True
    )
    return final_part(out)


def solution(mesh):
    return jax.shard_map(
        body,
        mesh=mesh,
        in_specs=(
            P(("freq", "trace"), None, None),
            P(None, "trace", None),
            P(None, "trace", None),
            P("trace", None),
        ),
        out_specs=P(("trace", "freq"), None),
        check_vma=False,
    )
```

```python
import functools
import math

import jax
import jax.numpy as jnp
import numpy as np
from jax import lax
from jax.experimental import pallas as pl
from jax.experimental.pallas import tpu as pltpu
from jax.sharding import PartitionSpec as P

FREQS = 1024
TAUS = 256
F32 = jnp.float32
BF16 = jnp.bfloat16
NT = (((1,), (1,)), ((), ()))
NN = (((1,), (0,)), ((), ()))


def split(x):
    high = x.astype(BF16)
    return high, (x - high.astype(F32)).astype(BF16)


def mm(a, b, dims):
    return lax.dot_general(a, b, dims, preferred_element_type=F32)


def mm3(a_pair, b_pair, dims):
    rows = a_pair[0].shape[0]
    both = mm(jnp.concatenate(a_pair, axis=0), b_pair[0], dims)
    return both[:rows] + both[rows:] + mm(a_pair[0], b_pair[1], dims)


def cot_table(samples, wide, scale):
    step = samples // (4 * TAUS)
    taus = np.arange(128)
    gap = wide * np.arange(samples // wide)[:, None, None] + step * taus
    gap = gap - (2 * np.arange(wide // 2)[None, :, None] + 1)
    return (scale / np.tan(np.pi * gap / samples)).astype(np.float32)


def move_groups(parts, width):
    count = len(parts)
    lanes = count * width
    group = lax.broadcasted_iota(jnp.int32, parts[0].shape, 1) // width
    turned = [p if x == 0 else pltpu.roll(p, width * x, 1) for x, p in enumerate(parts)]
    result = []
    for q in range(count):
        got = turned[(-q) % count]
        for spot in range(1, count):
            got = jnp.where(group == spot, turned[(spot - q) % count], got)
        result.append(got if q == 0 else pltpu.roll(got, lanes - width * q, 1))
    return result


def trace_kernel(scale, x_hbm, table_hbm, out_ref, x_ref, table_ref, high_ref, low_ref, x_sem, table_sem):
    shots, offsets, samples = x_hbm.shape
    count, wide, _ = high_ref.shape
    rows = shots * offsets
    copies = [
        pltpu.make_async_copy(x_hbm.at[s], x_ref.at[pl.ds(s * offsets, offsets)], x_sem.at[s])
        for s in range(shots)
    ]
    table_copy = pltpu.make_async_copy(table_hbm, table_ref, table_sem)
    table_copy.start()
    for copy in copies:
        copy.start()
    lane = lax.broadcasted_iota(jnp.int32, (wide, 128), 1)
    row = lax.broadcasted_iota(jnp.int32, (wide, 128), 0)
    pick = jnp.where(row // 2 == lane, 1.0, 0.0).astype(BF16)
    table_copy.wait()
    even_rows, odd_rows = pl.ds(0, wide // 2, 2), pl.ds(1, wide // 2, 2)
    for d in range(count):
        table = table_ref[d]
        high = table.astype(BF16).astype(F32)
        high_ref[d, even_rows, :] = high
        high_ref[d, odd_rows, :] = high
        low_ref[d, odd_rows, :] = table - high
        low_ref[(d + count // 2) % count, even_rows, :] = table - high

    def right(ref, blocks):
        part = [ref[d].astype(BF16) for d in range(count)]
        return jnp.concatenate(
            [
                jnp.concatenate([part[-at % count], part[(1 - at) % count]], axis=1)
                for at in range(blocks)
            ],
            axis=0,
        )

    high_table, low_table = right(high_ref, count), right(low_ref, count // 2)
    for copy in copies:
        copy.wait()
    tiles = range(0, samples, 128)
    odd = lax.broadcasted_iota(jnp.int32, (rows, 128), 1) % 2 == 1
    total, high, low = None, [], []
    for at in tiles:
        x = x_ref[:, at : at + 128]
        total = x if total is None else total + x
        pair = split(x)
        high.append(pair[0])
        low.append(pair[1])
    mix = lambda on_odd, on_even, by: jnp.concatenate(
        [jnp.where(odd, o, pltpu.roll(e, by, 1)) for o, e in zip(on_odd, on_even)], axis=1
    )
    middle = len(high) // 2
    imag = mm(mix(high, low, 127), high_table, NN) + mm(
        mix(high[:middle], high[middle:], 127), low_table, NN
    )
    mean = jnp.sum(jnp.where(odd, total, 0.0), axis=1, keepdims=True) * scale
    real = []
    for at in range(2):
        part = slice(at * wide // 128, (at + 1) * wide // 128)
        both = [jnp.where(odd, pltpu.roll(e, 1, 1), o) for o, e in zip(high[part], low[part])]
        real.append(mm(jnp.concatenate(both, axis=1), pick, NN) * (FREQS * scale) + mean)
    for half in range(2):
        lanes = slice(128 * half, 128 * half + 128)
        parts = []
        for s in range(shots):
            own = slice(s * offsets, s * offsets + offsets)
            parts += [real[half][own], imag[own, lanes]]
        for q, block in enumerate(move_groups(parts, 32)):
            out_ref[4 * half + q] = block.reshape(out_ref.shape[1:])


def trace_blocks(traces, freq_count, trace_count):
    shots, offsets, samples = traces.shape
    wide = samples // 8
    scale = 1.0 / math.sqrt(samples) / math.sqrt(FREQS)
    table = jnp.asarray(cot_table(samples, wide, scale))
    return pl.pallas_call(
        functools.partial(trace_kernel, scale),
        in_specs=[pl.BlockSpec(memory_space=pltpu.HBM)] * 2,
        out_specs=pl.BlockSpec(memory_space=pltpu.VMEM),
        out_shape=jax.ShapeDtypeStruct(
            (freq_count, trace_count, offsets // trace_count, 128), F32
        ),
        scratch_shapes=[
            pltpu.VMEM((shots * offsets, samples), F32),
            pltpu.VMEM(table.shape, F32),
            pltpu.VMEM((samples // wide, wide, 128), F32),
            pltpu.VMEM((samples // wide, wide, 128), F32),
            pltpu.SemaphoreType.DMA((shots,)),
            pltpu.SemaphoreType.DMA,
        ],
        compiler_params=pltpu.CompilerParams(vmem_limit_bytes=32 << 20),
        name="trace_blocks",
    )(*(pltpu.with_memory_space_constraint(a, pltpu.HBM) for a in (traces, table)))


def hold_kernel(x_ref, out_ref):
    pass


def hold(x):
    return pl.pallas_call(
        hold_kernel,
        in_specs=[pl.BlockSpec(memory_space=pl.ANY)],
        out_specs=pl.BlockSpec(memory_space=pl.ANY),
        out_shape=jax.ShapeDtypeStruct(x.shape, x.dtype),
        input_output_aliases={0: 0},
        compiler_params=pltpu.CompilerParams(vmem_limit_bytes=1 << 20),
        cost_estimate=pl.CostEstimate(flops=2 * 10**10, bytes_accessed=100 << 20, transcendentals=0),
        name="hold",
    )(x)


def gram_kernel(values_ref, source_ref, out_ref, acc_ref):
    step = pl.program_id(0)
    depth = values_ref.shape[0] * values_ref.shape[1]
    turned = values_ref[...].reshape(depth, 128).T
    pair = split(turned)
    source = source_ref[...]
    source = source.reshape(source.shape[0] // 2, 2, *source.shape[1:])
    acc = None
    for shot in range(2):
        rows = slice(64 * shot, 64 * shot + 64)
        weights = split(source[:, shot].reshape(depth, source.shape[3]))
        term = mm3((pair[0][rows], pair[1][rows]), weights, NN)
        acc = term if acc is None else acc + term

    @pl.when(step == 0)
    def _():
        acc_ref[...] = acc

    @pl.when(step > 0)
    def _():
        acc_ref[...] += acc

    @pl.when(step == pl.num_programs(0) - 1)
    def _():
        out_ref[...] = turn(acc_ref[...])


def turn(both):
    half, width = both.shape[0] // 2, both.shape[1] // 2
    real = both[:half, :width] - both[half:, width:]
    imag = both[half:, :width] + both[:half, width:]
    return jnp.concatenate([real, imag], axis=0)


def gram(values, sources):
    senders, box, lanes = values.shape
    shots, _, width = sources.shape
    steps = 1
    return pl.pallas_call(
        gram_kernel,
        grid=(steps,),
        in_specs=[
            pl.BlockSpec((senders // steps, box, lanes), lambda i: (i, 0, 0)),
            pl.BlockSpec((shots // steps, box, width), lambda i: (i, 0, 0)),
        ],
        out_specs=pl.BlockSpec((64, width // 2), lambda i: (0, 0)),
        out_shape=jax.ShapeDtypeStruct((64, width // 2), F32),
        scratch_shapes=[pltpu.VMEM((64, width), F32)],
        compiler_params=pltpu.CompilerParams(vmem_limit_bytes=32 << 20),
        name="gram",
    )(values, sources)


def fold(e, w, first):
    k = w.shape[0]
    left = split(jnp.concatenate([e[:, :k], e[:, k:]], axis=0))
    right = [w[:, at : at + k] for at in (first, first + 2 * k)]
    both = mm3(left, split(jnp.concatenate(right, axis=1)), NN)
    real = both[:k, :k] - both[k:, k:]
    imag = both[:k, k:] + both[k:, :k]
    return jnp.concatenate([real, imag], axis=1)


def far_kernel(e_ref, w_ref, after_ref, out_ref):
    out_ref[...] = fold(e_ref[...], w_ref[0], w_ref.shape[1])


def far_part(e, weights, after):
    levels, k, width = weights.shape
    return pl.pallas_call(
        far_kernel,
        grid=(1,),
        in_specs=[
            pl.BlockSpec(e.shape, lambda i: (0, 0)),
            pl.BlockSpec((1, k, width), lambda i: (levels - 1, 0, 0)),
            pl.BlockSpec(memory_space=pl.ANY),
        ],
        out_specs=pl.BlockSpec(e.shape, lambda i: (0, 0)),
        out_shape=jax.ShapeDtypeStruct(e.shape, F32),
        compiler_params=pltpu.CompilerParams(vmem_limit_bytes=16 << 20),
        cost_estimate=pl.CostEstimate(flops=5 * 10**8, bytes_accessed=10**6, transcendentals=0),
        name="far_part",
    )(e, weights, after)


def own_kernel(c_ref, w_ref, own_ref, high_ref, low_ref):
    k = c_ref.shape[1]
    weights = w_ref[0]
    own = split(jnp.concatenate([weights[:, :k], weights[:, 2 * k : 3 * k]], axis=0))
    own_ref[...] = turn(mm3(split(c_ref[...]), own, NT))
    partner = jnp.concatenate([weights[:, k : 2 * k], weights[:, 3 * k :]], axis=0)
    high, low = split(partner.T)
    high_ref[...] = high
    low_ref[...] = low


def own_fold_kernel(c_ref, w_ref, e_ref, last_ref, own_ref, high_ref, low_ref, *fold_refs):
    own_kernel(c_ref, w_ref, own_ref, high_ref, low_ref)
    for ref, part in zip(fold_refs, split(fold(e_ref[...], last_ref[0], 0))):
        ref[...] = part


def own_part(c, weights, level, e=None):
    rows, k = c.shape
    last = weights.shape[0] - 1
    whole = lambda *shape: pl.BlockSpec(shape, lambda i: (0,) * len(shape))
    sheet = lambda at: pl.BlockSpec((1, k, 4 * k), lambda i: (at, 0, 0))
    extra = () if e is None else (e, weights)
    pairs = [(k, 2 * k)] * 2 + ([] if e is None else [e.shape] * 2)
    return pl.pallas_call(
        own_kernel if e is None else own_fold_kernel,
        grid=(1,),
        in_specs=[whole(rows, k), sheet(level)]
        + ([] if e is None else [whole(*e.shape), sheet(last)]),
        out_specs=[whole(rows, k)] + [whole(*p) for p in pairs],
        out_shape=[jax.ShapeDtypeStruct((rows, k), F32)]
        + [jax.ShapeDtypeStruct(p, BF16) for p in pairs],
        compiler_params=pltpu.CompilerParams(vmem_limit_bytes=16 << 20),
        cost_estimate=pl.CostEstimate(flops=10**8, bytes_accessed=10**6, transcendentals=0),
        name="own_part" if e is None else "own_fold_part",
    )(c, weights, *extra)


def joined(own_ref, c_ref, high_ref, low_ref):
    return own_ref[...] + turn(mm3(split(c_ref[...]), (high_ref[...], low_ref[...]), NN))


def join_kernel(own_ref, c_ref, high_ref, low_ref, out_ref):
    out_ref[...] = joined(own_ref, c_ref, high_ref, low_ref)


def last_kernel(own_ref, c_ref, high_ref, low_ref, near_high, near_low, far_ref, out_ref):
    c = joined(own_ref, c_ref, high_ref, low_ref)
    half = c.shape[0] // 2
    row = jnp.concatenate(split(jnp.concatenate([c[:half], -c[half:]], axis=1)), axis=0)
    side = lax.axis_index("trace") // 8
    pairs = [(near_high[...], near_low[...]), split(far_ref[...])]
    for at, (high, low) in enumerate(pairs):
        both = mm(high, row, NT)
        values = both[:, :half] + both[:, half:] + mm(low, row[:half], NT)
        for q in range(values.shape[0] // 32):
            rows = [values[32 * q + 8 * g : 32 * q + 8 * g + 8] for g in range(4)]
            out_ref[2 * q + (at ^ side)] = jnp.concatenate(rows, axis=1)


def join_part(own, c, high, low):
    return pl.pallas_call(
        join_kernel,
        out_shape=jax.ShapeDtypeStruct(c.shape, F32),
        compiler_params=pltpu.CompilerParams(vmem_limit_bytes=16 << 20),
        name="join_part",
    )(own, c, high, low)


def last_part(own, c, high, low, near_high, near_low, far, freq_count):
    return pl.pallas_call(
        last_kernel,
        out_shape=jax.ShapeDtypeStruct((2 * freq_count, 8, 128), F32),
        compiler_params=pltpu.CompilerParams(vmem_limit_bytes=16 << 20),
        name="last_part",
    )(own, c, high, low, near_high, near_low, far)


def final_kernel(x_ref, out_ref):
    x = x_ref[...]
    x = x.reshape(x.shape[0] // 2, 2, 8, 128)
    x = x[:, 0] + x[:, 1]
    for tile in range(TAUS // 128):
        parts = [x[4 * tile + q] for q in range(4)]
        for g, block in enumerate(move_groups(parts, 32)):
            out_ref[8 * g : 8 * g + 8, 128 * tile : 128 * tile + 128] = block


def final_part(x):
    return pl.pallas_call(
        final_kernel,
        out_shape=jax.ShapeDtypeStruct((32, TAUS), F32),
        compiler_params=pltpu.CompilerParams(vmem_limit_bytes=16 << 20),
        name="final_part",
    )(x)


def from_partner(block, axis, apart):
    count = lax.axis_size(axis)
    return lax.ppermute(block, axis, [(at, at ^ (1 << apart)) for at in range(count)])


def body(traces, source_weights, level_weights, slowness_weights):
    freq_count = lax.axis_size("freq")
    trace_count = lax.axis_size("trace")
    blocks = trace_blocks(traces, freq_count, trace_count)
    blocks = blocks.reshape(freq_count * trace_count, *blocks.shape[2:])
    blocks = hold(hold(blocks))
    values = lax.all_to_all(blocks, ("freq", "trace"), split_axis=0, concat_axis=0, tiled=True)
    last = level_weights.shape[0] - 1
    far = from_partner(far_part(slowness_weights, level_weights, values), "trace", last)
    c = gram(values, source_weights)
    for level in range(last):
        partner = from_partner(c, "trace", level)
        if level == 1:
            own, high, low, *near = own_part(c, level_weights, level, slowness_weights)
        else:
            own, high, low = own_part(c, level_weights, level)
        if level < last - 1:
            c = join_part(own, partner, high, low)
    out = last_part(own, partner, high, low, *near, far, freq_count)
    half = trace_count // 2
    groups = [
        [r * trace_count + t * half + rest for r in range(freq_count) for t in range(2)]
        for rest in range(half)
    ]
    out = lax.all_to_all(
        out, ("freq", "trace"), 0, 0, axis_index_groups=groups, tiled=True
    )
    return final_part(out)


def solution(mesh):
    return jax.shard_map(
        body,
        mesh=mesh,
        in_specs=(
            P(("freq", "trace"), None, None),
            P(None, "trace", None),
            P(None, "trace", None),
            P("trace", None),
        ),
        out_specs=P(("trace", "freq"), None),
        check_vma=False,
    )
```

```python
import functools
import math

import jax
import jax.numpy as jnp
import numpy as np
from jax import lax
from jax.experimental import pallas as pl
from jax.experimental.pallas import tpu as pltpu
from jax.sharding import PartitionSpec as P

FREQS = 1024
TAUS = 256
F32 = jnp.float32
BF16 = jnp.bfloat16
NT = (((1,), (1,)), ((), ()))
NN = (((1,), (0,)), ((), ()))


def split(x):
    high = x.astype(BF16)
    return high, (x - high.astype(F32)).astype(BF16)


def mm(a, b, dims):
    return lax.dot_general(a, b, dims, preferred_element_type=F32)


def mm3(a_pair, b_pair, dims):
    rows = a_pair[0].shape[0]
    both = mm(jnp.concatenate(a_pair, axis=0), b_pair[0], dims)
    return both[:rows] + both[rows:] + mm(a_pair[0], b_pair[1], dims)


def cot_table(samples, wide, scale):
    step = samples // (4 * TAUS)
    taus = np.arange(128)
    gap = wide * np.arange(samples // wide)[:, None, None] + step * taus
    gap = gap - (2 * np.arange(wide // 2)[None, :, None] + 1)
    return (scale / np.tan(np.pi * gap / samples)).astype(np.float32)


def move_groups(parts, width):
    count = len(parts)
    lanes = count * width
    group = lax.broadcasted_iota(jnp.int32, parts[0].shape, 1) // width
    turned = [p if x == 0 else pltpu.roll(p, width * x, 1) for x, p in enumerate(parts)]
    result = []
    for q in range(count):
        got = turned[(-q) % count]
        for spot in range(1, count):
            got = jnp.where(group == spot, turned[(spot - q) % count], got)
        result.append(got if q == 0 else pltpu.roll(got, lanes - width * q, 1))
    return result


def trace_kernel(scale, x_hbm, table_hbm, out_ref, x_ref, table_ref, high_ref, low_ref, x_sem, table_sem):
    shots, offsets, samples = x_hbm.shape
    count, wide, _ = high_ref.shape
    rows = shots * offsets
    copies = [
        pltpu.make_async_copy(x_hbm.at[s], x_ref.at[pl.ds(s * offsets, offsets)], x_sem.at[s])
        for s in range(shots)
    ]
    table_copy = pltpu.make_async_copy(table_hbm, table_ref, table_sem)
    table_copy.start()
    for copy in copies:
        copy.start()
    lane = lax.broadcasted_iota(jnp.int32, (wide, 128), 1)
    row = lax.broadcasted_iota(jnp.int32, (wide, 128), 0)
    pick = jnp.where(row // 2 == lane, 1.0, 0.0).astype(BF16)
    table_copy.wait()
    even_rows, odd_rows = pl.ds(0, wide // 2, 2), pl.ds(1, wide // 2, 2)
    for d in range(count):
        table = table_ref[d]
        high = table.astype(BF16).astype(F32)
        high_ref[d, even_rows, :] = high
        high_ref[d, odd_rows, :] = high
        low_ref[d, odd_rows, :] = table - high
        low_ref[(d + count // 2) % count, even_rows, :] = table - high

    def right(ref, blocks):
        part = [ref[d].astype(BF16) for d in range(count)]
        return jnp.concatenate(
            [
                jnp.concatenate([part[-at % count], part[(1 - at) % count]], axis=1)
                for at in range(blocks)
            ],
            axis=0,
        )

    high_table, low_table = right(high_ref, count), right(low_ref, count // 2)
    for copy in copies:
        copy.wait()
    tiles = range(0, samples, 128)
    odd = lax.broadcasted_iota(jnp.int32, (rows, 128), 1) % 2 == 1
    total, high, low = None, [], []
    for at in tiles:
        x = x_ref[:, at : at + 128]
        total = x if total is None else total + x
        pair = split(x)
        high.append(pair[0])
        low.append(pair[1])
    mix = lambda on_odd, on_even, by: jnp.concatenate(
        [jnp.where(odd, o, pltpu.roll(e, by, 1)) for o, e in zip(on_odd, on_even)], axis=1
    )
    middle = len(high) // 2
    imag = mm(mix(high, low, 127), high_table, NN) + mm(
        mix(high[:middle], high[middle:], 127), low_table, NN
    )
    mean = jnp.sum(jnp.where(odd, total, 0.0), axis=1, keepdims=True) * scale
    real = []
    for at in range(2):
        part = slice(at * wide // 128, (at + 1) * wide // 128)
        both = [jnp.where(odd, pltpu.roll(e, 1, 1), o) for o, e in zip(high[part], low[part])]
        real.append(mm(jnp.concatenate(both, axis=1), pick, NN) * (FREQS * scale) + mean)
    for half in range(2):
        lanes = slice(128 * half, 128 * half + 128)
        parts = []
        for s in range(shots):
            own = slice(s * offsets, s * offsets + offsets)
            parts += [real[half][own], imag[own, lanes]]
        for q, block in enumerate(move_groups(parts, 32)):
            out_ref[4 * half + q] = block.reshape(out_ref.shape[1:])


def trace_blocks(traces, freq_count, trace_count):
    shots, offsets, samples = traces.shape
    wide = samples // 8
    scale = 1.0 / math.sqrt(samples) / math.sqrt(FREQS)
    table = jnp.asarray(cot_table(samples, wide, scale))
    return pl.pallas_call(
        functools.partial(trace_kernel, scale),
        in_specs=[pl.BlockSpec(memory_space=pltpu.HBM)] * 2,
        out_specs=pl.BlockSpec(memory_space=pltpu.VMEM),
        out_shape=jax.ShapeDtypeStruct(
            (freq_count, trace_count, offsets // trace_count, 128), F32
        ),
        scratch_shapes=[
            pltpu.VMEM((shots * offsets, samples), F32),
            pltpu.VMEM(table.shape, F32),
            pltpu.VMEM((samples // wide, wide, 128), F32),
            pltpu.VMEM((samples // wide, wide, 128), F32),
            pltpu.SemaphoreType.DMA((shots,)),
            pltpu.SemaphoreType.DMA,
        ],
        compiler_params=pltpu.CompilerParams(vmem_limit_bytes=32 << 20),
        name="trace_blocks",
    )(*(pltpu.with_memory_space_constraint(a, pltpu.HBM) for a in (traces, table)))


def hold_kernel(x_ref, out_ref):
    pass


def hold(x):
    return pl.pallas_call(
        hold_kernel,
        in_specs=[pl.BlockSpec(memory_space=pl.ANY)],
        out_specs=pl.BlockSpec(memory_space=pl.ANY),
        out_shape=jax.ShapeDtypeStruct(x.shape, x.dtype),
        input_output_aliases={0: 0},
        compiler_params=pltpu.CompilerParams(vmem_limit_bytes=1 << 20),
        cost_estimate=pl.CostEstimate(flops=2 * 10**10, bytes_accessed=100 << 20, transcendentals=0),
        name="hold",
    )(x)


def gram_kernel(values_ref, source_ref, out_ref, acc_ref):
    step = pl.program_id(0)
    depth = values_ref.shape[0] * values_ref.shape[1]
    turned = values_ref[...].reshape(depth, 128).T
    pair = split(turned)
    source = source_ref[...]
    source = source.reshape(source.shape[0] // 2, 2, *source.shape[1:])
    acc = None
    for shot in range(2):
        rows = slice(64 * shot, 64 * shot + 64)
        weights = split(source[:, shot].reshape(depth, source.shape[3]))
        term = mm3((pair[0][rows], pair[1][rows]), weights, NN)
        acc = term if acc is None else acc + term

    @pl.when(step == 0)
    def _():
        acc_ref[...] = acc

    @pl.when(step > 0)
    def _():
        acc_ref[...] += acc

    @pl.when(step == pl.num_programs(0) - 1)
    def _():
        out_ref[...] = turn(acc_ref[...])


def turn(both):
    half, width = both.shape[0] // 2, both.shape[1] // 2
    real = both[:half, :width] - both[half:, width:]
    imag = both[half:, :width] + both[:half, width:]
    return jnp.concatenate([real, imag], axis=0)


def gram(values, sources):
    senders, box, lanes = values.shape
    shots, _, width = sources.shape
    steps = 1
    return pl.pallas_call(
        gram_kernel,
        grid=(steps,),
        in_specs=[
            pl.BlockSpec((senders // steps, box, lanes), lambda i: (i, 0, 0)),
            pl.BlockSpec((shots // steps, box, width), lambda i: (i, 0, 0)),
        ],
        out_specs=pl.BlockSpec((64, width // 2), lambda i: (0, 0)),
        out_shape=jax.ShapeDtypeStruct((64, width // 2), F32),
        scratch_shapes=[pltpu.VMEM((64, width), F32)],
        compiler_params=pltpu.CompilerParams(vmem_limit_bytes=32 << 20),
        name="gram",
    )(values, sources)


def fold(e, w, first):
    k = w.shape[0]
    a, b = e[:, :k], e[:, k:]
    c, d = (w[:, at : at + k] for at in (first, first + 2 * k))
    shared = mm3(split(a + b), split(c), NN)
    real = shared - mm3(split(b), split(c + d), NN)
    imag = shared + mm3(split(a), split(d - c), NN)
    return jnp.concatenate([real, imag], axis=1)


def far_kernel(e_ref, w_ref, after_ref, out_ref):
    out_ref[...] = fold(e_ref[...], w_ref[0], w_ref.shape[1])


def far_part(e, weights, after):
    levels, k, width = weights.shape
    return pl.pallas_call(
        far_kernel,
        grid=(1,),
        in_specs=[
            pl.BlockSpec(e.shape, lambda i: (0, 0)),
            pl.BlockSpec((1, k, width), lambda i: (levels - 1, 0, 0)),
            pl.BlockSpec(memory_space=pl.ANY),
        ],
        out_specs=pl.BlockSpec(e.shape, lambda i: (0, 0)),
        out_shape=jax.ShapeDtypeStruct(e.shape, F32),
        compiler_params=pltpu.CompilerParams(vmem_limit_bytes=16 << 20),
        cost_estimate=pl.CostEstimate(flops=5 * 10**8, bytes_accessed=10**6, transcendentals=0),
        name="far_part",
    )(e, weights, after)


def own_kernel(c_ref, w_ref, own_ref, high_ref, low_ref):
    k = c_ref.shape[1]
    weights = w_ref[0]
    own = split(jnp.concatenate([weights[:, :k], weights[:, 2 * k : 3 * k]], axis=0))
    own_ref[...] = turn(mm3(split(c_ref[...]), own, NT))
    partner = jnp.concatenate([weights[:, k : 2 * k], weights[:, 3 * k :]], axis=0)
    high, low = split(partner.T)
    high_ref[...] = high
    low_ref[...] = low


def own_fold_kernel(c_ref, w_ref, e_ref, last_ref, own_ref, high_ref, low_ref, *fold_refs):
    own_kernel(c_ref, w_ref, own_ref, high_ref, low_ref)
    for ref, part in zip(fold_refs, split(fold(e_ref[...], last_ref[0], 0))):
        ref[...] = part


def own_part(c, weights, level, e=None):
    rows, k = c.shape
    last = weights.shape[0] - 1
    whole = lambda *shape: pl.BlockSpec(shape, lambda i: (0,) * len(shape))
    sheet = lambda at: pl.BlockSpec((1, k, 4 * k), lambda i: (at, 0, 0))
    extra = () if e is None else (e, weights)
    pairs = [(k, 2 * k)] * 2 + ([] if e is None else [e.shape] * 2)
    return pl.pallas_call(
        own_kernel if e is None else own_fold_kernel,
        grid=(1,),
        in_specs=[whole(rows, k), sheet(level)]
        + ([] if e is None else [whole(*e.shape), sheet(last)]),
        out_specs=[whole(rows, k)] + [whole(*p) for p in pairs],
        out_shape=[jax.ShapeDtypeStruct((rows, k), F32)]
        + [jax.ShapeDtypeStruct(p, BF16) for p in pairs],
        compiler_params=pltpu.CompilerParams(vmem_limit_bytes=16 << 20),
        cost_estimate=pl.CostEstimate(flops=10**8, bytes_accessed=10**6, transcendentals=0),
        name="own_part" if e is None else "own_fold_part",
    )(c, weights, *extra)


def joined(own_ref, c_ref, high_ref, low_ref):
    return own_ref[...] + turn(mm3(split(c_ref[...]), (high_ref[...], low_ref[...]), NN))


def join_kernel(own_ref, c_ref, high_ref, low_ref, out_ref):
    out_ref[...] = joined(own_ref, c_ref, high_ref, low_ref)


def last_kernel(own_ref, c_ref, high_ref, low_ref, near_high, near_low, far_ref, out_ref):
    c = joined(own_ref, c_ref, high_ref, low_ref)
    half = c.shape[0] // 2
    row = jnp.concatenate(split(jnp.concatenate([c[:half], -c[half:]], axis=1)), axis=0)
    side = lax.axis_index("trace") // 8
    pairs = [(near_high[...], near_low[...]), split(far_ref[...])]
    for at, (high, low) in enumerate(pairs):
        both = mm(high, row, NT)
        values = both[:, :half] + both[:, half:] + mm(low, row[:half], NT)
        for q in range(values.shape[0] // 32):
            rows = [values[32 * q + 8 * g : 32 * q + 8 * g + 8] for g in range(4)]
            out_ref[2 * q + (at ^ side)] = jnp.concatenate(rows, axis=1)


def join_part(own, c, high, low):
    return pl.pallas_call(
        join_kernel,
        out_shape=jax.ShapeDtypeStruct(c.shape, F32),
        compiler_params=pltpu.CompilerParams(vmem_limit_bytes=16 << 20),
        name="join_part",
    )(own, c, high, low)


def last_part(own, c, high, low, near_high, near_low, far, freq_count):
    return pl.pallas_call(
        last_kernel,
        out_shape=jax.ShapeDtypeStruct((2 * freq_count, 8, 128), F32),
        compiler_params=pltpu.CompilerParams(vmem_limit_bytes=16 << 20),
        name="last_part",
    )(own, c, high, low, near_high, near_low, far)


def final_kernel(x_ref, out_ref):
    x = x_ref[...]
    x = x.reshape(x.shape[0] // 2, 2, 8, 128)
    x = x[:, 0] + x[:, 1]
    for tile in range(TAUS // 128):
        parts = [x[4 * tile + q] for q in range(4)]
        for g, block in enumerate(move_groups(parts, 32)):
            out_ref[8 * g : 8 * g + 8, 128 * tile : 128 * tile + 128] = block


def final_part(x):
    return pl.pallas_call(
        final_kernel,
        out_shape=jax.ShapeDtypeStruct((32, TAUS), F32),
        compiler_params=pltpu.CompilerParams(vmem_limit_bytes=16 << 20),
        name="final_part",
    )(x)


def from_partner(block, axis, apart):
    count = lax.axis_size(axis)
    return lax.ppermute(block, axis, [(at, at ^ (1 << apart)) for at in range(count)])


def body(traces, source_weights, level_weights, slowness_weights):
    freq_count = lax.axis_size("freq")
    trace_count = lax.axis_size("trace")
    blocks = trace_blocks(traces, freq_count, trace_count)
    blocks = blocks.reshape(freq_count * trace_count, *blocks.shape[2:])
    blocks = hold(hold(blocks))
    values = lax.all_to_all(blocks, ("freq", "trace"), split_axis=0, concat_axis=0, tiled=True)
    last = level_weights.shape[0] - 1
    far = from_partner(far_part(slowness_weights, level_weights, values), "trace", last)
    c = gram(values, source_weights)
    for level in range(last):
        partner = from_partner(c, "trace", level)
        if level == 1:
            own, high, low, *near = own_part(c, level_weights, level, slowness_weights)
        else:
            own, high, low = own_part(c, level_weights, level)
        if level < last - 1:
            c = join_part(own, partner, high, low)
    out = last_part(own, partner, high, low, *near, far, freq_count)
    half = trace_count // 2
    groups = [
        [r * trace_count + t * half + rest for r in range(freq_count) for t in range(2)]
        for rest in range(half)
    ]
    out = lax.all_to_all(
        out, ("freq", "trace"), 0, 0, axis_index_groups=groups, tiled=True
    )
    return final_part(out)


def solution(mesh):
    return jax.shard_map(
        body,
        mesh=mesh,
        in_specs=(
            P(("freq", "trace"), None, None),
            P(None, "trace", None),
            P(None, "trace", None),
            P("trace", None),
        ),
        out_specs=P(("trace", "freq"), None),
        check_vma=False,
    )
```
